32 devices in a mesh: aux: 4 (over y, core), orb: 8 (over z, x).
Axes of the slice: x: 2, y: 2, z: 4, core: 2. Of those that a mesh axis runs over, the one named last changes fastest.
Arguments:
- integrals: float32 [2048, 16, 512], P('aux', 'orb'), may hold values from -0.6 to 0.6
- metric: float32 [2048, 2048], P('aux'), may hold values from -1 to 3, as said below
- occ_energy: float32 [16], replicated, may hold values from -1.2 to -0.2
- vir_energy: float32 [512], replicated, may hold values from 0.1 to 2
- pair_orbitals: int32 [128, 2], replicated, may hold values from 0 to 15, as said below
Outputs:
- gradient: float32 [2048, 16, 512], P('aux', 'orb')
The draws below stay inside these ranges and needn't reach their ends.
Inputs may be any that keep to these rules, and one draw needn't show every extreme that they name: metric is exactly symmetric. `pair_orbitals`: the pairs of one patch use at most one orbital from the block of 2 orbitals of each orb index.
All inputs are finite; a program needn't handle non-finite values.
Results may differ from the reference program's by a relative error of at most 0.0003.
Values sent between devices are 32-bit elements; how exact they have to be, the bound alone decides.
A program may use at most 128 MiB of HBM per device.

```python
import jax
import jax.numpy as jnp
from jax import lax

NV = 512
NAUX = 2048
OCC_DEV = 2
PAIR_DEV = 16
NOCC = 16
N_ORB = 8


def draw_metric(key, part):
    key_diag = jax.random.fold_in(key, 11)
    key_off = jax.random.fold_in(key, 12)
    diagonal = jax.random.uniform(key_diag, (NAUX,), jnp.float32, 0.5, 2.0)
    raw_values = jax.random.normal(key_off, (NAUX, NAUX), jnp.float32) * 0.012
    off_diag = (raw_values + raw_values.T) * 0.5
    identity = jnp.eye(NAUX, dtype=bool)
    return jnp.where(identity, diagonal[:, None], off_diag).astype(jnp.float32)


def draw_pair_orbitals(key, part):
    key_pick = jax.random.fold_in(key, 21)
    key_near = jax.random.fold_in(key, 22)
    key_far = jax.random.fold_in(key, 23)
    pick_table = jax.random.randint(key_pick, (N_ORB, N_ORB), 0, OCC_DEV)
    owner_dev = jnp.arange(N_ORB, dtype=jnp.int32)[:, None]
    near_dev = jnp.clip(owner_dev + jax.random.randint(key_near, (N_ORB, PAIR_DEV), -2, 3), 0, N_ORB - 1)
    far_dev = jax.random.randint(key_far, (N_ORB, PAIR_DEV), 0, N_ORB)
    first_orb = near_dev * OCC_DEV + jnp.take_along_axis(pick_table, near_dev, axis=1)
    second_orb = far_dev * OCC_DEV + jnp.take_along_axis(pick_table, far_dev, axis=1)
    return jnp.stack([first_orb, second_orb], -1).reshape(N_ORB * PAIR_DEV, 2).astype(jnp.int32)


def level_of(own_key, shape, shards, low, high):
    def one(axis_at, blocks):
        steps = jax.random.uniform(jax.random.fold_in(jax.random.fold_in(own_key, 6), axis_at), (blocks,), jnp.float32, low / len(shards), high / len(shards))
        return jnp.repeat(jnp.exp(steps), shape[axis_at] // blocks).reshape((-1,) + (1,) * (len(shape) - axis_at - 1))

    gain = one(*shards[0])
    for cut in shards[1:]:
        gain = gain * one(*cut)
    return gain


def centred(stream_key, shape, spread, reach, split=(), kind=jnp.bfloat16):
    array = jax.random.normal(stream_key, shape, jnp.float32) * spread
    if len(split) > 0:
        array = level_of(stream_key, shape, split, -0.22, 0.18) * array
    return jnp.clip(array, min=-reach, max=reach).astype(kind)


def setup_inputs(seed: int = 0) -> dict:
    keys = jax.random.split(jax.random.key(seed), 6)
    integrals = centred(keys[0], (NAUX, NOCC, NV), 0.1, 0.6, ((0, 4), (1, 8)), jnp.float32)
    metric = draw_metric(jax.random.fold_in(keys[5], 71), 0)
    occ_energy = jnp.clip(jax.random.uniform(keys[2], (NOCC,), jnp.float32, -1.2, -0.2), -1.2, -0.2)
    vir_energy = jnp.clip(jax.random.uniform(keys[3], (NV,), jnp.float32, 0.1, 2.0), 0.1, 2.0)
    pair_orbitals = draw_pair_orbitals(jax.random.fold_in(keys[5], 71), 0)
    return dict(integrals=integrals, metric=metric, occ_energy=occ_energy, vir_energy=vir_energy, pair_orbitals=pair_orbitals)


def reference(integrals, metric, occ_energy, vir_energy, pair_orbitals):
    aux_total, occ_total, vir_total = integrals.shape
    flat_rows = integrals.reshape(aux_total, occ_total * vir_total)
    fitted = jnp.dot(metric.T, flat_rows, precision=lax.Precision.HIGHEST, preferred_element_type=jnp.float32)
    fitted = fitted.reshape(aux_total, occ_total, vir_total)

    def visit_pair(grads, pair_row):
        first_orb = pair_row[0].astype(jnp.int32)
        second_orb = pair_row[1].astype(jnp.int32)
        left_block = lax.dynamic_index_in_dim(fitted, first_orb, 1, keepdims=False)
        right_block = lax.dynamic_index_in_dim(fitted, second_orb, 1, keepdims=False)
        coupling = jnp.dot(left_block.T, right_block, precision=lax.Precision.HIGHEST, preferred_element_type=jnp.float32)
        denominator = vir_energy[:, None] + vir_energy[None, :] - occ_energy[first_orb] - occ_energy[second_orb]
        amplitudes = -coupling / denominator
        to_first = jnp.dot(right_block, amplitudes.T, precision=lax.Precision.HIGHEST, preferred_element_type=jnp.float32)
        to_second = jnp.dot(left_block, amplitudes, precision=lax.Precision.HIGHEST, preferred_element_type=jnp.float32)
        grads = grads.at[:, first_orb].add(to_first)
        grads = grads.at[:, second_orb].add(to_second)
        return grads, None

    start_grads = jnp.zeros((aux_total, occ_total, vir_total), jnp.float32)
    grads, _ = lax.scan(visit_pair, start_grads, pair_orbitals)
    return grads
```

```python
import functools

import jax
import jax.numpy as jnp
from jax import lax
from jax.experimental import pallas as pl
from jax.experimental.pallas import tpu as pltpu
from jax.sharding import PartitionSpec as P

high = lax.Precision.HIGH
MESH = pl.DeviceIdType.MESH
VMEM_LIMIT = 60 * 1024 * 1024
f32 = jnp.float32
bf16 = jnp.bfloat16


def flip(index, step, count):
    total = 0
    bit = 1
    while bit < count:
        total = total + bit * ((index // bit + (step // bit) % 2) % 2)
        bit *= 2
    return total


def spread_order(count):
    far = list(range(count // 2, count))
    near = list(range(1, count // 2))
    far = far[0::2] + far[1::2]
    merged = []
    while far or near:
        if far:
            merged.append(far.pop(0))
        if near:
            merged.append(near.pop(0))
    return merged


def split(value):
    upper = value.astype(bf16)
    lower = (value - upper.astype(f32)).astype(bf16)
    return upper, lower


def dot3(left, right, dims):
    lu, ll = split(left)
    ru, rl = split(right)
    mul = functools.partial(
        lax.dot_general, dimension_numbers=(dims, ((), ())), preferred_element_type=f32
    )
    return mul(lu, ru) + (mul(lu, rl) + mul(ll, ru))


def gather_kernel(
    orb_count,
    y_count,
    exchange,
    x_ref,
    out_ref,
    stage,
    local_sem,
    orb_send,
    orb_recv,
    y_send,
    y_recv,
    c_send,
    c_recv,
):
    aux = lax.axis_index("aux")
    orb = lax.axis_index("orb")
    y = aux // 2
    core = aux % 2
    partner = 2 * y + 1 - core
    blocks = x_ref.shape[0]

    def y_peer(j):
        return 2 * ((y + j) % y_count) + core

    barrier = pltpu.get_barrier_semaphore()
    greeted = 0
    if exchange:
        for k in range(1, orb_count):
            pl.semaphore_signal(
                barrier,
                inc=1,
                device_id={"aux": aux, "orb": flip(orb, k, orb_count)},
                device_id_type=MESH,
            )
            greeted += 1
    for j in range(1, y_count):
        pl.semaphore_signal(
            barrier, inc=1, device_id={"aux": y_peer(j), "orb": orb}, device_id_type=MESH
        )
        greeted += 1
    pl.semaphore_signal(
        barrier, inc=1, device_id={"aux": partner, "orb": orb}, device_id_type=MESH
    )
    greeted += 1
    pl.semaphore_wait(barrier, greeted)

    def orb_copy(k):
        to = flip(orb, k, orb_count)
        return pltpu.make_async_remote_copy(
            src_ref=x_ref.at[to],
            dst_ref=out_ref.at[aux, orb],
            send_sem=orb_send.at[k],
            recv_sem=orb_recv.at[k],
            device_id={"aux": aux, "orb": to},
            device_id_type=MESH,
        )

    def own(k):
        if not exchange:
            return x_ref.at[k], k
        place = flip(orb, k, orb_count)
        if k == 0:
            return x_ref.at[place], place
        return out_ref.at[aux, place], place

    def y_copy(k, j):
        src, place = own(k)
        return pltpu.make_async_remote_copy(
            src_ref=src,
            dst_ref=out_ref.at[aux, place],
            send_sem=y_send.at[j - 1, k],
            recv_sem=y_recv.at[j - 1, k],
            device_id={"aux": y_peer(j), "orb": orb},
            device_id_type=MESH,
        )

    def core_copy(k):
        src, place = own(k)
        return pltpu.make_async_remote_copy(
            src_ref=src,
            dst_ref=out_ref.at[aux, place],
            send_sem=c_send.at[0, k],
            recv_sem=c_recv.at[0, k],
            device_id={"aux": partner, "orb": orb},
            device_id_type=MESH,
        )

    def relay_copy(k, j):
        source = 2 * ((y + y_count - j) % y_count) + core
        place = own(k)[1]
        return pltpu.make_async_remote_copy(
            src_ref=out_ref.at[source, place],
            dst_ref=out_ref.at[source, place],
            send_sem=c_send.at[j, k],
            recv_sem=c_recv.at[j, k],
            device_id={"aux": partner, "orb": orb},
            device_id_type=MESH,
        )

    steps = spread_order(orb_count) if exchange else list(range(1, blocks))
    if exchange:
        for k in steps:
            orb_copy(k).start()
    pending = []

    def relay(k):
        for j in range(1, y_count):
            y_copy(k, j).wait_recv()
            relay_copy(k, j).start()

    for k in [0] + steps:
        if exchange and k:
            orb_copy(k).wait_recv()
        for j in range(1, y_count):
            y_copy(k, j).start()
        core_copy(k).start()
        if k == 0 or not exchange:
            src, place = own(k)
            load = pltpu.make_async_copy(src, stage, local_sem)
            load.start()
            load.wait()
            save = pltpu.make_async_copy(stage, out_ref.at[aux, place], local_sem)
            save.start()
            save.wait()
        pending.append(k)
        if len(pending) > 2:
            relay(pending.pop(0))
    for k in pending:
        relay(k)
    for k in [0] + steps:
        core_copy(k).wait()
        for j in range(1, y_count):
            relay_copy(k, j).wait()
            y_copy(k, j).wait_send()
        if exchange and k:
            orb_copy(k).wait_send()


def gather(blocks, aux_count, exchange, collective_id):
    count = blocks.shape[0]
    y_count = aux_count // 2
    dma = pltpu.SemaphoreType.DMA
    return pl.pallas_call(
        functools.partial(gather_kernel, count, y_count, exchange),
        out_shape=jax.ShapeDtypeStruct((aux_count,) + blocks.shape, f32),
        in_specs=[pl.BlockSpec(memory_space=pl.ANY)],
        out_specs=pl.BlockSpec(memory_space=pl.ANY),
        scratch_shapes=[
            pltpu.VMEM(blocks.shape[1:], f32),
            dma(()),
            dma((count,)),
            dma((count,)),
            dma((y_count - 1, count)),
            dma((y_count - 1, count)),
            dma((y_count, count)),
            dma((y_count, count)),
        ],
        compiler_params=pltpu.CompilerParams(
            collective_id=collective_id, has_side_effects=True, vmem_limit_bytes=VMEM_LIMIT
        ),
        name="gather_exchange" if exchange else "gather_aux",
    )(blocks)


def return_kernel(
    orb_count,
    r_ref,
    out_ref,
    mine,
    theirs,
    sums,
    peer_sums,
    load_sem,
    c_send,
    c_recv,
    y_send,
    y_recv,
    orb_send,
    orb_recv,
    local_sem,
):
    aux = lax.axis_index("aux")
    orb = lax.axis_index("orb")
    y = aux // 2
    core = aux % 2
    partner = 2 * y + 1 - core
    across = 2 * (1 - y) + core
    rows = r_ref.shape[2]
    tile = 64

    barrier = pltpu.get_barrier_semaphore()
    for k in range(1, orb_count):
        pl.semaphore_signal(
            barrier,
            inc=1,
            device_id={"aux": aux, "orb": flip(orb, k, orb_count)},
            device_id_type=MESH,
        )
    for peer in (partner, across):
        pl.semaphore_signal(
            barrier, inc=1, device_id={"aux": peer, "orb": orb}, device_id_type=MESH
        )
    pl.semaphore_wait(barrier, orb_count + 1)

    half = orb_count // 2
    steps = list(range(half, orb_count, 2)) + list(range(half + 1, orb_count, 2))
    steps = steps + list(range(half - 1, 0, -1)) + [0]

    def core_copy(k, side):
        row = y if side == 0 else 1 - y
        return pltpu.make_async_remote_copy(
            src_ref=r_ref.at[2 * row + 1 - core, flip(orb, k, orb_count)],
            dst_ref=theirs.at[side, k],
            send_sem=c_send.at[side, k],
            recv_sem=c_recv.at[side, k],
            device_id={"aux": partner, "orb": orb},
            device_id_type=MESH,
        )

    def load(k, side, slot):
        row = y if side == 0 else 1 - y
        return pltpu.make_async_copy(
            r_ref.at[2 * row + core, flip(orb, k, orb_count)],
            mine.at[slot, side],
            load_sem.at[slot, side],
        )

    def y_copy(k):
        return pltpu.make_async_remote_copy(
            src_ref=sums.at[1, k],
            dst_ref=peer_sums.at[k],
            send_sem=y_send.at[k],
            recv_sem=y_recv.at[k],
            device_id={"aux": across, "orb": orb},
            device_id_type=MESH,
        )

    def orb_copy(k):
        return pltpu.make_async_remote_copy(
            src_ref=sums.at[0, k],
            dst_ref=out_ref.at[orb],
            send_sem=orb_send.at[k],
            recv_sem=orb_recv.at[k],
            device_id={"aux": aux, "orb": flip(orb, k, orb_count)},
            device_id_type=MESH,
        )

    def add(into, left, right):
        def one(i, carry):
            at = pl.ds(pl.multiple_of(i * tile, tile), tile)
            into[at, :] = left[at, :] + right[at, :]
            return carry

        lax.fori_loop(0, rows // tile, one, 0)

    def finish(k):
        y_copy(k).wait_recv()
        add(sums.at[0, k], sums.at[0, k], peer_sums.at[k])
        if k:
            orb_copy(k).start()

    for k in steps:
        for side in (1, 0):
            core_copy(k, side).start()
    for side in (1, 0):
        load(steps[0], side, 0).start()
    pending = []
    for place, k in enumerate(steps):
        slot = place % 2
        if place + 1 < len(steps):
            for side in (1, 0):
                load(steps[place + 1], side, 1 - slot).start()
        for side in (1, 0):
            core_copy(k, side).wait_recv()
            load(k, side, slot).wait()
            add(sums.at[side, k], mine.at[slot, side], theirs.at[side, k])
            if side == 1:
                y_copy(k).start()
        pending.append(k)
        if len(pending) > 2:
            finish(pending.pop(0))
    for k in pending:
        finish(k)
    keep = pltpu.make_async_copy(sums.at[0, 0], out_ref.at[orb], local_sem)
    keep.start()
    keep.wait()
    for k in steps:
        for side in (1, 0):
            core_copy(k, side).wait_send()
        y_copy(k).wait_send()
        if k:
            orb_copy(k).wait()


def give_back(contributions, collective_id):
    _, orb_count, rows, cols = contributions.shape
    dma = pltpu.SemaphoreType.DMA
    return pl.pallas_call(
        functools.partial(return_kernel, orb_count),
        out_shape=jax.ShapeDtypeStruct((orb_count, rows, cols), f32),
        in_specs=[pl.BlockSpec(memory_space=pl.ANY)],
        out_specs=pl.BlockSpec(memory_space=pl.ANY),
        scratch_shapes=[
            pltpu.VMEM((2, 2, rows, cols), f32),
            pltpu.VMEM((2, orb_count, rows, cols), f32),
            pltpu.VMEM((2, orb_count, rows, cols), f32),
            pltpu.VMEM((orb_count, rows, cols), f32),
            dma((2, 2)),
            dma((2, orb_count)),
            dma((2, orb_count)),
            dma((orb_count,)),
            dma((orb_count,)),
            dma((orb_count,)),
            dma((orb_count,)),
            dma(()),
        ],
        compiler_params=pltpu.CompilerParams(
            collective_id=collective_id, has_side_effects=True, vmem_limit_bytes=VMEM_LIMIT
        ),
        name="give_back",
    )(contributions)


def amplitude_kernel(first_ref, second_ref, shift_ref, left, right, col, row, out, total):
    pair = pl.program_id(0)
    step = pl.program_id(1)

    @pl.when(step == 0)
    def _():
        total[...] = jnp.zeros_like(total)

    total[...] += dot3(left[0, 0], right[0, 0], ((0,), (0,)))

    @pl.when(step == pl.num_programs(1) - 1)
    def _():
        out[0] = -total[...] / (col[...] + row[...] - shift_ref[pair])


def amplitudes_of(first_slot, second_slot, shift, slots, vir_energy):
    pairs = first_slot.shape[0]
    aux_count, _, rows, cols = slots.shape
    return pl.pallas_call(
        amplitude_kernel,
        grid_spec=pltpu.PrefetchScalarGridSpec(
            num_scalar_prefetch=3,
            grid=(pairs, aux_count),
            in_specs=[
                pl.BlockSpec((1, 1, rows, cols), lambda p, a, f, s, e: (a, f[p], 0, 0)),
                pl.BlockSpec((1, 1, rows, cols), lambda p, a, f, s, e: (a, s[p], 0, 0)),
                pl.BlockSpec((cols, 1), lambda p, a, f, s, e: (0, 0)),
                pl.BlockSpec((1, cols), lambda p, a, f, s, e: (0, 0)),
            ],
            out_specs=pl.BlockSpec((1, cols, cols), lambda p, a, f, s, e: (p, 0, 0)),
            scratch_shapes=[pltpu.VMEM((cols, cols), f32)],
        ),
        out_shape=jax.ShapeDtypeStruct((pairs, cols, cols), f32),
        compiler_params=pltpu.CompilerParams(vmem_limit_bytes=VMEM_LIMIT),
        name="pair_amplitudes",
    )(first_slot, second_slot, shift, slots, slots, vir_energy[:, None], vir_energy[None, :])


def contribution_kernel(first_ref, second_ref, slots, amps, out):
    slot = pl.program_id(1)
    out[0, 0] = jnp.zeros_like(out[0, 0])

    def visit(pair, carry):
        first = first_ref[pair]
        second = second_ref[pair]

        @pl.when(first == slot)
        def _():
            out[0, 0] += dot3(slots[0, second], amps[pair], ((1,), (1,)))

        @pl.when(second == slot)
        def _():
            out[0, 0] += dot3(slots[0, first], amps[pair], ((1,), (0,)))

        return carry

    lax.fori_loop(0, amps.shape[0], visit, 0)


def contributions_of(first_slot, second_slot, slots, amps):
    aux_count, orb_count, rows, cols = slots.shape
    return pl.pallas_call(
        contribution_kernel,
        grid_spec=pltpu.PrefetchScalarGridSpec(
            num_scalar_prefetch=2,
            grid=(aux_count, orb_count),
            in_specs=[
                pl.BlockSpec((1, orb_count, rows, cols), lambda a, o, f, s: (a, 0, 0, 0)),
                pl.BlockSpec(amps.shape, lambda a, o, f, s: (0, 0, 0)),
            ],
            out_specs=pl.BlockSpec((1, 1, rows, cols), lambda a, o, f, s: (a, o, 0, 0)),
        ),
        out_shape=jax.ShapeDtypeStruct(slots.shape, f32),
        compiler_params=pltpu.CompilerParams(vmem_limit_bytes=VMEM_LIMIT),
        name="slot_contributions",
    )(first_slot, second_slot, slots, amps)


def body(integrals, metric, occ_energy, vir_energy, pair_orbitals):
    aux_rows, occ_count, vir_count = integrals.shape
    aux_count = lax.axis_size("aux")
    orb_count = lax.axis_size("orb")
    aux_index = lax.axis_index("aux")
    orb_index = lax.axis_index("orb")
    pieces = 4
    columns = occ_count * vir_count
    all_rows = gather(
        integrals.reshape(pieces, aux_rows // pieces, columns), aux_count, False, 1
    ).reshape(aux_count * aux_rows, columns)
    fitted = lax.dot_general(
        metric, all_rows, (((1,), (0,)), ((), ())), precision=high, preferred_element_type=f32
    )
    pair_count = pair_orbitals.shape[0] // orb_count
    pair_ends = pair_orbitals.reshape(orb_count, 2 * pair_count)
    local_pick = jnp.where(pair_ends // occ_count == orb_index, pair_ends % occ_count, -1)
    wanted = jnp.max(local_pick, axis=1)
    outgoing = jnp.zeros((orb_count, aux_rows, vir_count), f32)
    for o in range(occ_count):
        part = fitted[:, o * vir_count : (o + 1) * vir_count]
        outgoing = jnp.where((wanted == o)[:, None, None], part[None], outgoing)
    slots = gather(outgoing, aux_count, True, 2)
    my_count = pair_count // aux_count
    my_pairs = lax.dynamic_slice_in_dim(
        pair_orbitals, orb_index * pair_count + aux_index * my_count, my_count, 0
    )
    first_orb = my_pairs[:, 0]
    second_orb = my_pairs[:, 1]
    first_slot = first_orb // occ_count
    second_slot = second_orb // occ_count
    shift = occ_energy[first_orb] + occ_energy[second_orb]
    amps = amplitudes_of(first_slot, second_slot, shift, slots, vir_energy)
    contributions = contributions_of(first_slot, second_slot, slots, amps)
    received = give_back(contributions, 3)
    outs = [
        jnp.sum(jnp.where((wanted == o)[:, None, None], received, 0.0), axis=0)
        for o in range(occ_count)
    ]
    return jnp.stack(outs, axis=1)


def plain_body(integrals, metric, occ_energy, vir_energy, pair_orbitals):
    aux_rows, occ_count, vir_count = integrals.shape
    flat_rows = integrals.reshape(aux_rows, occ_count * vir_count)
    fitted = lax.psum_scatter(
        lax.dot_general(
            metric, flat_rows, (((0,), (0,)), ((), ())), precision=high, preferred_element_type=f32
        ),
        "aux",
        scatter_dimension=0,
        tiled=True,
    )
    fitted = fitted.reshape(aux_rows, occ_count, vir_count)
    orb_count = lax.axis_size("orb")
    my_index = lax.axis_index("orb")
    pair_count = pair_orbitals.shape[0] // orb_count
    pair_ends = pair_orbitals.reshape(orb_count, 2 * pair_count)
    local_pick = jnp.where(pair_ends // occ_count == my_index, pair_ends % occ_count, -1)
    wanted = jnp.max(local_pick, axis=1)
    chooser = (wanted[:, None] == jnp.arange(occ_count, dtype=jnp.int32)[None, :]).astype(f32)
    outgoing = jnp.einsum("to,qoa->qta", chooser, fitted, precision=high)
    arrived = lax.all_to_all(outgoing, "orb", split_axis=1, concat_axis=1, tiled=True)
    my_pairs = lax.dynamic_slice_in_dim(pair_orbitals, my_index * pair_count, pair_count, 0)
    first_orb = my_pairs[:, 0]
    second_orb = my_pairs[:, 1]
    first_slot = first_orb // occ_count
    second_slot = second_orb // occ_count
    left_block = jnp.take(arrived, first_slot, axis=1)
    right_block = jnp.take(arrived, second_slot, axis=1)
    partial_sums = jnp.einsum("qpa,qpb->pab", left_block, right_block, precision=high)
    occ_shift = occ_energy[first_orb] + occ_energy[second_orb]
    amp_share = lax.psum_scatter(partial_sums, "aux", scatter_dimension=1, tiled=True)
    share_rows = amp_share.shape[1]
    part_vir = lax.dynamic_slice_in_dim(
        vir_energy, lax.axis_index("aux") * share_rows, share_rows, 0
    )
    denominator = part_vir[None, :, None] + vir_energy[None, None, :] - occ_shift[:, None, None]
    amplitudes = lax.all_gather(-amp_share / denominator, "aux", axis=1, tiled=True)
    to_first = jnp.einsum("qpb,pab->qpa", right_block, amplitudes, precision=high)
    to_second = jnp.einsum("qpa,pab->qpb", left_block, amplitudes, precision=high)
    slot_ids = jnp.arange(orb_count, dtype=jnp.int32)
    first_hits = (first_slot[:, None] == slot_ids[None, :]).astype(f32)
    second_hits = (second_slot[:, None] == slot_ids[None, :]).astype(f32)
    return_slots = jnp.einsum("qpa,ps->qsa", to_first, first_hits, precision=high)
    return_slots = return_slots + jnp.einsum(
        "qpa,ps->qsa", to_second, second_hits, precision=high
    )
    received = lax.all_to_all(return_slots, "orb", split_axis=1, concat_axis=1, tiled=True)
    return jnp.einsum("qta,to->qoa", received, chooser, precision=high)


def solution(mesh):
    aux_count = mesh.shape["aux"]
    orb_count = mesh.shape["orb"]

    def step(integrals, metric, occ_energy, vir_energy, pair_orbitals):
        slot_bytes = 4 * metric.shape[1] * integrals.shape[2] * orb_count
        fits = 2 * slot_bytes <= 64 * 1024 * 1024
        power = orb_count & (orb_count - 1) == 0
        whole_pairs = pair_orbitals.shape[0] % (orb_count * aux_count) == 0
        chosen = body if fits and power and whole_pairs and aux_count == 4 else plain_body
        return jax.shard_map(
            chosen,
            mesh=mesh,
            in_specs=(P("aux", "orb", None), P("aux", None), P(), P(), P()),
            out_specs=P("aux", "orb", None),
            check_vma=False,
        )(integrals, metric, occ_energy, vir_energy, pair_orbitals)

    return step
```

```python
import functools

import jax
import jax.numpy as jnp
from jax import lax
from jax.experimental import pallas as pl
from jax.experimental.pallas import tpu as pltpu
from jax.sharding import PartitionSpec as P

high = lax.Precision.HIGH
MESH = pl.DeviceIdType.MESH
VMEM_LIMIT = 60 * 1024 * 1024
f32 = jnp.float32
bf16 = jnp.bfloat16


def flip(index, step, count):
    total = 0
    bit = 1
    while bit < count:
        total = total + bit * ((index // bit + (step // bit) % 2) % 2)
        bit *= 2
    return total


def spread_order(count):
    far = list(range(count // 2, count))
    near = list(range(2, count // 2))
    far = far[0::2] + far[1::2]
    merged = [1]
    while far or near:
        if far:
            merged.append(far.pop(0))
        if near:
            merged.append(near.pop(0))
    return merged


def split(value):
    upper = value.astype(bf16)
    lower = (value - upper.astype(f32)).astype(bf16)
    return upper, lower


def dot3(left, right, dims):
    (lu, ll), (ru, rl) = left, right
    (la,), (ra,) = dims
    return lax.dot_general(
        jnp.concatenate([lu, lu, ll], axis=la),
        jnp.concatenate([ru, rl, ru], axis=ra),
        (dims, ((), ())),
        preferred_element_type=f32,
    )


def gather_kernel(
    orb_count,
    y_count,
    exchange,
    x_ref,
    out_ref,
    stage,
    keep_sem,
    orb_send,
    orb_recv,
    y_send,
    y_recv,
    c_send,
    c_recv,
):
    aux = lax.axis_index("aux")
    orb = lax.axis_index("orb")
    y = aux // 2
    core = aux % 2
    partner = 2 * y + 1 - core
    blocks = x_ref.shape[0]

    def y_peer(j):
        return 2 * ((y + j) % y_count) + core

    barrier = pltpu.get_barrier_semaphore()
    greeted = 0
    if exchange:
        for k in range(1, orb_count):
            pl.semaphore_signal(
                barrier,
                inc=1,
                device_id={"aux": aux, "orb": flip(orb, k, orb_count)},
                device_id_type=MESH,
            )
            greeted += 1
    for j in range(1, y_count):
        pl.semaphore_signal(
            barrier, inc=1, device_id={"aux": y_peer(j), "orb": orb}, device_id_type=MESH
        )
        greeted += 1
    pl.semaphore_signal(
        barrier, inc=1, device_id={"aux": partner, "orb": orb}, device_id_type=MESH
    )
    greeted += 1
    pl.semaphore_wait(barrier, greeted)

    def orb_copy(k, h):
        to = flip(orb, k, orb_count)
        return pltpu.make_async_remote_copy(
            src_ref=x_ref.at[to, h],
            dst_ref=out_ref.at[aux, orb, h],
            send_sem=orb_send.at[k, h],
            recv_sem=orb_recv.at[k, h],
            device_id={"aux": aux, "orb": to},
            device_id_type=MESH,
        )

    def place_of(k):
        return flip(orb, k, orb_count) if exchange else k

    def own(k, h):
        if not exchange or k == 0:
            return x_ref.at[place_of(k), h]
        return out_ref.at[aux, place_of(k), h]

    def y_copy(k, h, j):
        return pltpu.make_async_remote_copy(
            src_ref=own(k, h),
            dst_ref=out_ref.at[aux, place_of(k), h],
            send_sem=y_send.at[j - 1, k, h],
            recv_sem=y_recv.at[j - 1, k, h],
            device_id={"aux": y_peer(j), "orb": orb},
            device_id_type=MESH,
        )

    def core_copy(k, h):
        return pltpu.make_async_remote_copy(
            src_ref=own(k, h),
            dst_ref=out_ref.at[aux, place_of(k), h],
            send_sem=c_send.at[0, k, h],
            recv_sem=c_recv.at[0, k, h],
            device_id={"aux": partner, "orb": orb},
            device_id_type=MESH,
        )

    def relay_copy(k, h, j):
        source = 2 * ((y + y_count - j) % y_count) + core
        return pltpu.make_async_remote_copy(
            src_ref=out_ref.at[source, place_of(k), h],
            dst_ref=out_ref.at[source, place_of(k), h],
            send_sem=c_send.at[j, k, h],
            recv_sem=c_recv.at[j, k, h],
            device_id={"aux": partner, "orb": orb},
            device_id_type=MESH,
        )

    steps = spread_order(orb_count) if exchange else list(range(1, blocks))
    units = [(k, h) for k in [0] + steps for h in range(x_ref.shape[1])]
    if exchange:
        for k, h in units:
            if k:
                orb_copy(k, h).start()
    pending = []

    def relay(k, h):
        for j in range(1, y_count):
            y_copy(k, h, j).wait_recv()
            relay_copy(k, h, j).start()

    def keep_loads():
        return [
            pltpu.make_async_copy(own(k, h), stage.at[i], keep_sem.at[i])
            for i, (k, h) in enumerate(keeps)
        ]

    def keep_saves():
        return [
            pltpu.make_async_copy(stage.at[i], out_ref.at[aux, place_of(k), h], keep_sem.at[i])
            for i, (k, h) in enumerate(keeps)
        ]

    keeps = [(k, h) for k, h in units if k == 0 or not exchange]
    for copy in keep_loads():
        copy.start()
    for index, (k, h) in enumerate(units):
        if exchange and k:
            orb_copy(k, h).wait_recv()
        for j in range(1, y_count):
            y_copy(k, h, j).start()
        core_copy(k, h).start()
        pending.append((k, h))
        if len(pending) > 2:
            relay(*pending.pop(0))
        if index == len(keeps) - 1:
            for load, save in zip(keep_loads(), keep_saves()):
                load.wait()
                save.start()
    for unit in pending:
        relay(*unit)
    for k, h in units:
        core_copy(k, h).wait()
        for j in range(1, y_count):
            relay_copy(k, h, j).wait()
            y_copy(k, h, j).wait_send()
        if exchange and k:
            orb_copy(k, h).wait_send()
    for save in keep_saves():
        save.wait()


def gather(blocks, aux_count, exchange, collective_id):
    count, parts = blocks.shape[:2]
    y_count = aux_count // 2
    kept = parts if exchange else count * parts
    dma = pltpu.SemaphoreType.DMA
    return pl.pallas_call(
        functools.partial(gather_kernel, count, y_count, exchange),
        out_shape=jax.ShapeDtypeStruct((aux_count,) + blocks.shape, f32),
        in_specs=[pl.BlockSpec(memory_space=pl.ANY)],
        out_specs=pl.BlockSpec(memory_space=pl.ANY),
        scratch_shapes=[
            pltpu.VMEM((kept,) + blocks.shape[2:], f32),
            dma((kept,)),
            dma((count, parts)),
            dma((count, parts)),
            dma((y_count - 1, count, parts)),
            dma((y_count - 1, count, parts)),
            dma((y_count, count, parts)),
            dma((y_count, count, parts)),
        ],
        compiler_params=pltpu.CompilerParams(
            collective_id=collective_id, has_side_effects=True, vmem_limit_bytes=VMEM_LIMIT
        ),
        name="gather_exchange" if exchange else "gather_aux",
    )(blocks)


def return_kernel(
    orb_count,
    r_ref,
    out_ref,
    mine,
    theirs,
    sums,
    peer_sums,
    load_sem,
    c_send,
    c_recv,
    y_send,
    y_recv,
    orb_send,
    orb_recv,
    keep_sem,
):
    aux = lax.axis_index("aux")
    orb = lax.axis_index("orb")
    y = aux // 2
    core = aux % 2
    partner = 2 * y + 1 - core
    across = 2 * (1 - y) + core
    parts, rows = r_ref.shape[2:4]
    tile = 64

    barrier = pltpu.get_barrier_semaphore()
    for k in range(1, orb_count):
        pl.semaphore_signal(
            barrier,
            inc=1,
            device_id={"aux": aux, "orb": flip(orb, k, orb_count)},
            device_id_type=MESH,
        )
    for peer in (partner, across):
        pl.semaphore_signal(
            barrier, inc=1, device_id={"aux": peer, "orb": orb}, device_id_type=MESH
        )
    pl.semaphore_wait(barrier, orb_count + 1)

    steps = [(k, h) for k in spread_order(orb_count)[1:] + [1, 0] for h in range(parts)]

    def core_copy(k, h, side):
        row = y if side == 0 else 1 - y
        return pltpu.make_async_remote_copy(
            src_ref=r_ref.at[2 * row + 1 - core, flip(orb, k, orb_count), h],
            dst_ref=theirs.at[side, k, h],
            send_sem=c_send.at[side, k, h],
            recv_sem=c_recv.at[side, k, h],
            device_id={"aux": partner, "orb": orb},
            device_id_type=MESH,
        )

    def load(k, h, side, slot):
        row = y if side == 0 else 1 - y
        return pltpu.make_async_copy(
            r_ref.at[2 * row + core, flip(orb, k, orb_count), h],
            mine.at[slot, side],
            load_sem.at[slot, side],
        )

    def y_copy(k, h):
        return pltpu.make_async_remote_copy(
            src_ref=sums.at[1, k, h],
            dst_ref=peer_sums.at[k, h],
            send_sem=y_send.at[k, h],
            recv_sem=y_recv.at[k, h],
            device_id={"aux": across, "orb": orb},
            device_id_type=MESH,
        )

    def orb_copy(k, h):
        return pltpu.make_async_remote_copy(
            src_ref=sums.at[0, k, h],
            dst_ref=out_ref.at[orb, h],
            send_sem=orb_send.at[k, h],
            recv_sem=orb_recv.at[k, h],
            device_id={"aux": aux, "orb": flip(orb, k, orb_count)},
            device_id_type=MESH,
        )

    def keep(h):
        return pltpu.make_async_copy(sums.at[0, 0, h], out_ref.at[orb, h], keep_sem.at[h])

    def add(into, left, right):
        def one(i, carry):
            at = pl.ds(pl.multiple_of(i * tile, tile), tile)
            into[at, :] = left[at, :] + right[at, :]
            return carry

        lax.fori_loop(0, rows // tile, one, 0)

    def finish(k, h):
        y_copy(k, h).wait_recv()
        add(sums.at[0, k, h], sums.at[0, k, h], peer_sums.at[k, h])
        if k:
            orb_copy(k, h).start()
        else:
            keep(h).start()

    for k, h in steps:
        for side in (1, 0):
            core_copy(k, h, side).start()
    for side in (1, 0):
        load(*steps[0], side, 0).start()
    pending = []
    for place, (k, h) in enumerate(steps):
        slot = place % 2
        if place + 1 < len(steps):
            for side in (1, 0):
                load(*steps[place + 1], side, 1 - slot).start()
        for side in (1, 0):
            core_copy(k, h, side).wait_recv()
            load(k, h, side, slot).wait()
            add(sums.at[side, k, h], mine.at[slot, side], theirs.at[side, k, h])
            if side == 1:
                y_copy(k, h).start()
        pending.append((k, h))
        if len(pending) > 2:
            finish(*pending.pop(0))
    for unit in pending:
        finish(*unit)
    for k, h in steps:
        for side in (1, 0):
            core_copy(k, h, side).wait_send()
        y_copy(k, h).wait_send()
        if k:
            orb_copy(k, h).wait()
        else:
            keep(h).wait()


def give_back(contributions, collective_id):
    orb_count, parts, rows, cols = contributions.shape[1:]
    whole = (orb_count, parts, rows, cols)
    dma = pltpu.SemaphoreType.DMA
    return pl.pallas_call(
        functools.partial(return_kernel, orb_count),
        out_shape=jax.ShapeDtypeStruct(whole, f32),
        in_specs=[pl.BlockSpec(memory_space=pl.ANY)],
        out_specs=pl.BlockSpec(memory_space=pl.ANY),
        scratch_shapes=[
            pltpu.VMEM((2, 2, rows, cols), f32),
            pltpu.VMEM((2,) + whole, f32),
            pltpu.VMEM((2,) + whole, f32),
            pltpu.VMEM(whole, f32),
            dma((2, 2)),
            dma((2, orb_count, parts)),
            dma((2, orb_count, parts)),
            dma((orb_count, parts)),
            dma((orb_count, parts)),
            dma((orb_count, parts)),
            dma((orb_count, parts)),
            dma((parts,)),
        ],
        compiler_params=pltpu.CompilerParams(
            collective_id=collective_id, has_side_effects=True, vmem_limit_bytes=VMEM_LIMIT
        ),
        name="give_back",
    )(contributions)


def amplitude_kernel(
    first_ref, second_ref, shift_ref, left, right, col, row, upper, lower, total
):
    pair = pl.program_id(0)
    step = pl.program_id(1)

    @pl.when(step == 0)
    def _():
        total[...] = jnp.zeros_like(total)

    total[...] += dot3(split(left[0, 0]), split(right[0, 0]), ((0,), (0,)))

    @pl.when(step == pl.num_programs(1) - 1)
    def _():
        amps = -total[...] / (col[...] + row[...] - shift_ref[pair])
        upper[0], lower[0] = split(amps)


def amplitudes_of(first_slot, second_slot, shift, slots, vir_energy):
    pairs = first_slot.shape[0]
    aux_count, _, rows, cols = slots.shape
    return pl.pallas_call(
        amplitude_kernel,
        grid_spec=pltpu.PrefetchScalarGridSpec(
            num_scalar_prefetch=3,
            grid=(pairs, aux_count),
            in_specs=[
                pl.BlockSpec((1, 1, rows, cols), lambda p, a, f, s, e: (a, f[p], 0, 0)),
                pl.BlockSpec((1, 1, rows, cols), lambda p, a, f, s, e: (a, s[p], 0, 0)),
                pl.BlockSpec((cols, 1), lambda p, a, f, s, e: (0, 0)),
                pl.BlockSpec((1, cols), lambda p, a, f, s, e: (0, 0)),
            ],
            out_specs=[pl.BlockSpec((1, cols, cols), lambda p, a, f, s, e: (p, 0, 0))] * 2,
            scratch_shapes=[pltpu.VMEM((cols, cols), f32)],
        ),
        out_shape=[jax.ShapeDtypeStruct((pairs, cols, cols), bf16)] * 2,
        compiler_params=pltpu.CompilerParams(vmem_limit_bytes=VMEM_LIMIT),
        name="pair_amplitudes",
    )(first_slot, second_slot, shift, slots, slots, vir_energy[:, None], vir_energy[None, :])


def contribution_kernel(first_ref, second_ref, slots, upper, lower, out):
    slot = pl.program_id(1)
    out[0, 0] = jnp.zeros_like(out[0, 0])

    def visit(pair, carry):
        first = first_ref[pair]
        second = second_ref[pair]

        @pl.when(first == slot)
        def _():
            out[0, 0] += dot3(
                split(slots[0, second]), (upper[pair], lower[pair]), ((1,), (1,))
            )

        @pl.when(second == slot)
        def _():
            out[0, 0] += dot3(
                split(slots[0, first]), (upper[pair], lower[pair]), ((1,), (0,))
            )

        return carry

    lax.fori_loop(0, upper.shape[0], visit, 0)


def contributions_of(first_slot, second_slot, slots, amps):
    aux_count, orb_count, rows, cols = slots.shape
    return pl.pallas_call(
        contribution_kernel,
        grid_spec=pltpu.PrefetchScalarGridSpec(
            num_scalar_prefetch=2,
            grid=(aux_count, orb_count),
            in_specs=[
                pl.BlockSpec((1, orb_count, rows, cols), lambda a, o, f, s: (a, 0, 0, 0)),
                pl.BlockSpec(amps[0].shape, lambda a, o, f, s: (0, 0, 0)),
                pl.BlockSpec(amps[1].shape, lambda a, o, f, s: (0, 0, 0)),
            ],
            out_specs=pl.BlockSpec((1, 1, rows, cols), lambda a, o, f, s: (a, o, 0, 0)),
        ),
        out_shape=jax.ShapeDtypeStruct(slots.shape, f32),
        compiler_params=pltpu.CompilerParams(vmem_limit_bytes=VMEM_LIMIT),
        name="slot_contributions",
    )(first_slot, second_slot, slots, *amps)


def body(integrals, metric, occ_energy, vir_energy, pair_orbitals):
    aux_rows, occ_count, vir_count = integrals.shape
    aux_count = lax.axis_size("aux")
    orb_count = lax.axis_size("orb")
    aux_index = lax.axis_index("aux")
    orb_index = lax.axis_index("orb")
    pieces = 8
    halves = (2, aux_rows // 2, vir_count)
    columns = occ_count * vir_count
    all_rows = gather(
        integrals.reshape(pieces, 1, aux_rows // pieces, columns), aux_count, False, 1
    ).reshape(aux_count * aux_rows, columns)
    fitted = lax.dot_general(
        metric, all_rows, (((1,), (0,)), ((), ())), precision=high, preferred_element_type=f32
    )
    pair_count = pair_orbitals.shape[0] // orb_count
    pair_ends = pair_orbitals.reshape(orb_count, 2 * pair_count)
    local_pick = jnp.where(pair_ends // occ_count == orb_index, pair_ends % occ_count, -1)
    wanted = jnp.max(local_pick, axis=1)
    outgoing = jnp.zeros((orb_count, aux_rows, vir_count), f32)
    for o in range(occ_count):
        part = fitted[:, o * vir_count : (o + 1) * vir_count]
        outgoing = jnp.where((wanted == o)[:, None, None], part[None], outgoing)
    slots = gather(outgoing.reshape((orb_count,) + halves), aux_count, True, 2)
    slots = slots.reshape(aux_count, orb_count, aux_rows, vir_count)
    my_count = pair_count // aux_count
    my_pairs = lax.dynamic_slice_in_dim(
        pair_orbitals, orb_index * pair_count + aux_index * my_count, my_count, 0
    )
    first_orb = my_pairs[:, 0]
    second_orb = my_pairs[:, 1]
    first_slot = first_orb // occ_count
    second_slot = second_orb // occ_count
    shift = occ_energy[first_orb] + occ_energy[second_orb]
    amps = amplitudes_of(first_slot, second_slot, shift, slots, vir_energy)
    contributions = contributions_of(first_slot, second_slot, slots, amps)
    received = give_back(contributions.reshape((aux_count, orb_count) + halves), 3)
    received = received.reshape(orb_count, aux_rows, vir_count)
    outs = [
        jnp.sum(jnp.where((wanted == o)[:, None, None], received, 0.0), axis=0)
        for o in range(occ_count)
    ]
    return jnp.stack(outs, axis=1)


def plain_body(integrals, metric, occ_energy, vir_energy, pair_orbitals):
    aux_rows, occ_count, vir_count = integrals.shape
    flat_rows = integrals.reshape(aux_rows, occ_count * vir_count)
    fitted = lax.psum_scatter(
        lax.dot_general(
            metric, flat_rows, (((0,), (0,)), ((), ())), precision=high, preferred_element_type=f32
        ),
        "aux",
        scatter_dimension=0,
        tiled=True,
    )
    fitted = fitted.reshape(aux_rows, occ_count, vir_count)
    orb_count = lax.axis_size("orb")
    my_index = lax.axis_index("orb")
    pair_count = pair_orbitals.shape[0] // orb_count
    pair_ends = pair_orbitals.reshape(orb_count, 2 * pair_count)
    local_pick = jnp.where(pair_ends // occ_count == my_index, pair_ends % occ_count, -1)
    wanted = jnp.max(local_pick, axis=1)
    chooser = (wanted[:, None] == jnp.arange(occ_count, dtype=jnp.int32)[None, :]).astype(f32)
    outgoing = jnp.einsum("to,qoa->qta", chooser, fitted, precision=high)
    arrived = lax.all_to_all(outgoing, "orb", split_axis=1, concat_axis=1, tiled=True)
    my_pairs = lax.dynamic_slice_in_dim(pair_orbitals, my_index * pair_count, pair_count, 0)
    first_orb = my_pairs[:, 0]
    second_orb = my_pairs[:, 1]
    first_slot = first_orb // occ_count
    second_slot = second_orb // occ_count
    left_block = jnp.take(arrived, first_slot, axis=1)
    right_block = jnp.take(arrived, second_slot, axis=1)
    partial_sums = jnp.einsum("qpa,qpb->pab", left_block, right_block, precision=high)
    occ_shift = occ_energy[first_orb] + occ_energy[second_orb]
    amp_share = lax.psum_scatter(partial_sums, "aux", scatter_dimension=1, tiled=True)
    share_rows = amp_share.shape[1]
    part_vir = lax.dynamic_slice_in_dim(
        vir_energy, lax.axis_index("aux") * share_rows, share_rows, 0
    )
    denominator = part_vir[None, :, None] + vir_energy[None, None, :] - occ_shift[:, None, None]
    amplitudes = lax.all_gather(-amp_share / denominator, "aux", axis=1, tiled=True)
    to_first = jnp.einsum("qpb,pab->qpa", right_block, amplitudes, precision=high)
    to_second = jnp.einsum("qpa,pab->qpb", left_block, amplitudes, precision=high)
    slot_ids = jnp.arange(orb_count, dtype=jnp.int32)
    first_hits = (first_slot[:, None] == slot_ids[None, :]).astype(f32)
    second_hits = (second_slot[:, None] == slot_ids[None, :]).astype(f32)
    return_slots = jnp.einsum("qpa,ps->qsa", to_first, first_hits, precision=high)
    return_slots = return_slots + jnp.einsum(
        "qpa,ps->qsa", to_second, second_hits, precision=high
    )
    received = lax.all_to_all(return_slots, "orb", split_axis=1, concat_axis=1, tiled=True)
    return jnp.einsum("qta,to->qoa", received, chooser, precision=high)


def solution(mesh):
    aux_count = mesh.shape["aux"]
    orb_count = mesh.shape["orb"]

    def step(integrals, metric, occ_energy, vir_energy, pair_orbitals):
        slot_bytes = 4 * metric.shape[1] * integrals.shape[2] * orb_count
        fits = 2 * slot_bytes <= 64 * 1024 * 1024
        power = orb_count & (orb_count - 1) == 0
        whole_pairs = pair_orbitals.shape[0] % (orb_count * aux_count) == 0
        chosen = body if fits and power and whole_pairs and aux_count == 4 else plain_body
        return jax.shard_map(
            chosen,
            mesh=mesh,
            in_specs=(P("aux", "orb", None), P("aux", None), P(), P(), P()),
            out_specs=P("aux", "orb", None),
            check_vma=False,
        )(integrals, metric, occ_energy, vir_energy, pair_orbitals)

    return step
```

```python
import functools

import jax
import jax.numpy as jnp
from jax import lax
from jax.experimental import pallas as pl
from jax.experimental.pallas import tpu as pltpu
from jax.sharding import PartitionSpec as P

high = lax.Precision.HIGH
MESH = pl.DeviceIdType.MESH
VMEM_LIMIT = 60 * 1024 * 1024
f32 = jnp.float32
bf16 = jnp.bfloat16


def flip(index, step, count):
    total = 0
    bit = 1
    while bit < count:
        total = total + bit * ((index // bit + (step // bit) % 2) % 2)
        bit *= 2
    return total


def spread_order(count):
    far = list(range(count // 2, count))
    near = list(range(2, count // 2))
    far = far[0::2] + far[1::2]
    merged = [1]
    while far or near:
        if far:
            merged.append(far.pop(0))
        if near:
            merged.append(near.pop(0))
    return merged


def split(value):
    upper = value.astype(bf16)
    lower = (value - upper.astype(f32)).astype(bf16)
    return upper, lower


def dot3(left, right, dims):
    (lu, ll), (ru, rl) = left, right
    (la,), (ra,) = dims
    return lax.dot_general(
        jnp.concatenate([lu, lu, ll], axis=la),
        jnp.concatenate([ru, rl, ru], axis=ra),
        (dims, ((), ())),
        preferred_element_type=f32,
    )


def gather_kernel(
    orb_count,
    y_count,
    exchange,
    x_ref,
    out_ref,
    stage,
    keep_sem,
    orb_send,
    orb_recv,
    y_send,
    y_recv,
    c_send,
    c_recv,
):
    aux = lax.axis_index("aux")
    orb = lax.axis_index("orb")
    y = aux // 2
    core = aux % 2
    partner = 2 * y + 1 - core
    blocks = x_ref.shape[0]

    def y_peer(j):
        return 2 * ((y + j) % y_count) + core

    barrier = pltpu.get_barrier_semaphore()
    greeted = 0
    if exchange:
        for k in range(1, orb_count):
            pl.semaphore_signal(
                barrier,
                inc=1,
                device_id={"aux": aux, "orb": flip(orb, k, orb_count)},
                device_id_type=MESH,
            )
            greeted += 1
    for j in range(1, y_count):
        pl.semaphore_signal(
            barrier, inc=1, device_id={"aux": y_peer(j), "orb": orb}, device_id_type=MESH
        )
        greeted += 1
    pl.semaphore_signal(
        barrier, inc=1, device_id={"aux": partner, "orb": orb}, device_id_type=MESH
    )
    greeted += 1
    pl.semaphore_wait(barrier, greeted)

    def orb_copy(k, h):
        to = flip(orb, k, orb_count)
        return pltpu.make_async_remote_copy(
            src_ref=x_ref.at[to, h],
            dst_ref=out_ref.at[aux, orb, h],
            send_sem=orb_send.at[k, h],
            recv_sem=orb_recv.at[k, h],
            device_id={"aux": aux, "orb": to},
            device_id_type=MESH,
        )

    def place_of(k):
        return flip(orb, k, orb_count) if exchange else k

    def own(k, h):
        if not exchange or k == 0:
            return x_ref.at[place_of(k), h]
        return out_ref.at[aux, place_of(k), h]

    def y_copy(k, h, j):
        return pltpu.make_async_remote_copy(
            src_ref=own(k, h),
            dst_ref=out_ref.at[aux, place_of(k), h],
            send_sem=y_send.at[j - 1, k, h],
            recv_sem=y_recv.at[j - 1, k, h],
            device_id={"aux": y_peer(j), "orb": orb},
            device_id_type=MESH,
        )

    def core_copy(k, h):
        return pltpu.make_async_remote_copy(
            src_ref=own(k, h),
            dst_ref=out_ref.at[aux, place_of(k), h],
            send_sem=c_send.at[0, k, h],
            recv_sem=c_recv.at[0, k, h],
            device_id={"aux": partner, "orb": orb},
            device_id_type=MESH,
        )

    def relay_copy(k, h, j):
        source = 2 * ((y + y_count - j) % y_count) + core
        return pltpu.make_async_remote_copy(
            src_ref=out_ref.at[source, place_of(k), h],
            dst_ref=out_ref.at[source, place_of(k), h],
            send_sem=c_send.at[j, k, h],
            recv_sem=c_recv.at[j, k, h],
            device_id={"aux": partner, "orb": orb},
            device_id_type=MESH,
        )

    steps = spread_order(orb_count) if exchange else list(range(1, blocks))
    units = [(k, h) for k in [0] + steps for h in range(x_ref.shape[1])]
    if exchange:
        for k, h in units:
            if k:
                orb_copy(k, h).start()
    pending = []

    def relay(k, h):
        for j in range(1, y_count):
            y_copy(k, h, j).wait_recv()
            relay_copy(k, h, j).start()

    def keep_loads():
        return [
            pltpu.make_async_copy(own(k, h), stage.at[i], keep_sem.at[i])
            for i, (k, h) in enumerate(keeps)
        ]

    def keep_saves():
        return [
            pltpu.make_async_copy(stage.at[i], out_ref.at[aux, place_of(k), h], keep_sem.at[i])
            for i, (k, h) in enumerate(keeps)
        ]

    keeps = [(k, h) for k, h in units if k == 0 or not exchange]
    for copy in keep_loads():
        copy.start()
    for index, (k, h) in enumerate(units):
        if exchange and k:
            orb_copy(k, h).wait_recv()
        for j in range(1, y_count):
            y_copy(k, h, j).start()
        core_copy(k, h).start()
        pending.append((k, h))
        if len(pending) > 2:
            relay(*pending.pop(0))
        if index == len(keeps) - 1:
            for load, save in zip(keep_loads(), keep_saves()):
                load.wait()
                save.start()
    for unit in pending:
        relay(*unit)
    for k, h in units:
        core_copy(k, h).wait()
        for j in range(1, y_count):
            relay_copy(k, h, j).wait()
            y_copy(k, h, j).wait_send()
        if exchange and k:
            orb_copy(k, h).wait_send()
    for save in keep_saves():
        save.wait()


def gather(blocks, aux_count, exchange, collective_id):
    count, parts = blocks.shape[:2]
    y_count = aux_count // 2
    kept = parts if exchange else count * parts
    dma = pltpu.SemaphoreType.DMA
    return pl.pallas_call(
        functools.partial(gather_kernel, count, y_count, exchange),
        out_shape=jax.ShapeDtypeStruct((aux_count,) + blocks.shape, f32),
        in_specs=[pl.BlockSpec(memory_space=pl.ANY)],
        out_specs=pl.BlockSpec(memory_space=pl.ANY),
        scratch_shapes=[
            pltpu.VMEM((kept,) + blocks.shape[2:], f32),
            dma((kept,)),
            dma((count, parts)),
            dma((count, parts)),
            dma((y_count - 1, count, parts)),
            dma((y_count - 1, count, parts)),
            dma((y_count, count, parts)),
            dma((y_count, count, parts)),
        ],
        compiler_params=pltpu.CompilerParams(
            collective_id=collective_id, has_side_effects=True, vmem_limit_bytes=VMEM_LIMIT
        ),
        name="gather_exchange" if exchange else "gather_aux",
    )(blocks)


def gateway_kernel(
    hit_ref,
    fit_ref,
    x_ref,
    out_ref,
    both,
    picks,
    stage,
    keep_sem,
    f_send,
    f_recv,
    orb_send,
    orb_recv,
    y_send,
    y_recv,
    c_send,
    c_recv,
):
    aux = lax.axis_index("aux")
    orb = lax.axis_index("orb")
    y = aux // 2
    core = aux % 2
    partner = 2 * y + 1 - core
    across = 2 * (1 - y) + core
    occ_count, parts, rows, _ = fit_ref.shape
    gate = 6
    tile = 64
    passed = {1: 7, 2: 4, 3: 5}

    def place_of(k):
        return flip(orb, k, 8)

    barrier = pltpu.get_barrier_semaphore()
    for k in (1, 2, 3, gate):
        pl.semaphore_signal(
            barrier, inc=1, device_id={"aux": aux, "orb": place_of(k)}, device_id_type=MESH
        )
    for peer in (partner, across):
        pl.semaphore_signal(
            barrier, inc=1, device_id={"aux": peer, "orb": orb}, device_id_type=MESH
        )
    pl.semaphore_wait(barrier, 6)

    def far_copy(o, h):
        return pltpu.make_async_remote_copy(
            src_ref=fit_ref.at[o, h],
            dst_ref=both.at[o, h],
            send_sem=f_send.at[o, h],
            recv_sem=f_recv.at[o, h],
            device_id={"aux": aux, "orb": place_of(gate)},
            device_id_type=MESH,
        )

    def near_copy(k, h):
        return pltpu.make_async_remote_copy(
            src_ref=x_ref.at[k, h],
            dst_ref=out_ref.at[aux, orb, h],
            send_sem=orb_send.at[k, h],
            recv_sem=orb_recv.at[k, h],
            device_id={"aux": aux, "orb": place_of(k)},
            device_id_type=MESH,
        )

    def pass_copy(d, h):
        return pltpu.make_async_remote_copy(
            src_ref=picks.at[d, h],
            dst_ref=out_ref.at[aux, place_of(gate), h],
            send_sem=orb_send.at[passed[d], h],
            recv_sem=orb_recv.at[passed[d], h],
            device_id={"aux": aux, "orb": place_of(d)},
            device_id_type=MESH,
        )

    def own(k, h):
        if k == 0:
            return x_ref.at[0, h]
        if k == gate:
            return picks.at[0, h]
        return out_ref.at[aux, place_of(k), h]

    def y_copy(k, h):
        return pltpu.make_async_remote_copy(
            src_ref=own(k, h),
            dst_ref=out_ref.at[aux, place_of(k), h],
            send_sem=y_send.at[k, h],
            recv_sem=y_recv.at[k, h],
            device_id={"aux": across, "orb": orb},
            device_id_type=MESH,
        )

    def core_copy(k, h):
        return pltpu.make_async_remote_copy(
            src_ref=own(k, h),
            dst_ref=out_ref.at[aux, place_of(k), h],
            send_sem=c_send.at[0, k, h],
            recv_sem=c_recv.at[0, k, h],
            device_id={"aux": partner, "orb": orb},
            device_id_type=MESH,
        )

    def relay_copy(k, h):
        return pltpu.make_async_remote_copy(
            src_ref=out_ref.at[across, place_of(k), h],
            dst_ref=out_ref.at[across, place_of(k), h],
            send_sem=c_send.at[1, k, h],
            recv_sem=c_recv.at[1, k, h],
            device_id={"aux": partner, "orb": orb},
            device_id_type=MESH,
        )

    def load(h):
        return pltpu.make_async_copy(x_ref.at[0, h], stage.at[h], keep_sem.at[0, h])

    def save(h):
        return pltpu.make_async_copy(
            stage.at[h], out_ref.at[aux, place_of(0), h], keep_sem.at[0, h]
        )

    def save_pick(h):
        return pltpu.make_async_copy(
            picks.at[0, h], out_ref.at[aux, place_of(gate), h], keep_sem.at[1, h]
        )

    def pick(h):
        for o in range(occ_count):
            far_copy(o, h).wait_recv()
        for d in (2, 3, 1, 0):

            def one(i, carry, d=d):
                at = pl.ds(pl.multiple_of(i * tile, tile), tile)
                total = both[0, h, at, :] * hit_ref[d, 0]
                for o in range(1, occ_count):
                    total = total + both[o, h, at, :] * hit_ref[d, o]
                picks[d, h, at, :] = total
                return carry

            lax.fori_loop(0, rows // tile, one, 0)
            if d:
                pass_copy(d, h).start()
            else:
                save_pick(h).start()

    for h in range(parts):
        for o in range(occ_count):
            far_copy(o, h).start()
        for k in (1, 2, 3):
            near_copy(k, h).start()
        load(h).start()
    units = [(k, h) for k in (0, 1, 2, 3, gate, 7, 4, 5) for h in range(parts)]
    pending = []

    def relay(k, h):
        y_copy(k, h).wait_recv()
        relay_copy(k, h).start()

    for index, (k, h) in enumerate(units):
        if k in (1, 2, 3):
            near_copy(k, h).wait_recv()
        elif k in (4, 5, 7):
            pltpu.make_async_remote_copy(
                src_ref=own(k, h),
                dst_ref=own(k, h),
                send_sem=orb_send.at[k, h],
                recv_sem=orb_recv.at[k, h],
                device_id={"aux": aux, "orb": place_of(gate)},
                device_id_type=MESH,
            ).wait_recv()
        y_copy(k, h).start()
        core_copy(k, h).start()
        pending.append((k, h))
        if len(pending) > 3:
            relay(*pending.pop(0))
        if index % parts == parts - 1 and index // parts < parts:
            pick(index // parts)
        if index == parts - 1:
            for i in range(parts):
                load(i).wait()
                save(i).start()
    for unit in pending:
        relay(*unit)
    for h in range(parts):
        for o in range(occ_count):
            far_copy(o, h).wait_send()
        for k in (1, 2, 3):
            near_copy(k, h).wait_send()
            pass_copy(k, h).wait_send()
        save(h).wait()
        save_pick(h).wait()
    for k, h in units:
        core_copy(k, h).wait()
        relay_copy(k, h).wait()
        y_copy(k, h).wait_send()


def gateway_exchange(hits, fitted, near, collective_id):
    parts = near.shape[1]
    piece = near.shape[2:]
    dma = pltpu.SemaphoreType.DMA
    return pl.pallas_call(
        gateway_kernel,
        out_shape=jax.ShapeDtypeStruct((4, 8, parts) + piece, f32),
        in_specs=[
            pl.BlockSpec(memory_space=pltpu.SMEM),
            pl.BlockSpec(memory_space=pl.ANY),
            pl.BlockSpec(memory_space=pl.ANY),
        ],
        out_specs=pl.BlockSpec(memory_space=pl.ANY),
        scratch_shapes=[
            pltpu.VMEM(fitted.shape, f32),
            pltpu.VMEM((4, parts) + piece, f32),
            pltpu.VMEM((parts,) + piece, f32),
            dma((2, parts)),
            dma(fitted.shape[:2]),
            dma(fitted.shape[:2]),
            dma((8, parts)),
            dma((8, parts)),
            dma((8, parts)),
            dma((8, parts)),
            dma((2, 8, parts)),
            dma((2, 8, parts)),
        ],
        compiler_params=pltpu.CompilerParams(
            collective_id=collective_id, has_side_effects=True, vmem_limit_bytes=VMEM_LIMIT
        ),
        name="gateway_exchange",
    )(hits, fitted, near)


def return_kernel(
    orb_count,
    r_ref,
    out_ref,
    mine,
    theirs,
    sums,
    peer_sums,
    load_sem,
    c_send,
    c_recv,
    y_send,
    y_recv,
    orb_send,
    orb_recv,
    keep_sem,
):
    aux = lax.axis_index("aux")
    orb = lax.axis_index("orb")
    y = aux // 2
    core = aux % 2
    partner = 2 * y + 1 - core
    across = 2 * (1 - y) + core
    parts, rows = r_ref.shape[2:4]
    tile = 64

    barrier = pltpu.get_barrier_semaphore()
    for k in range(1, orb_count):
        pl.semaphore_signal(
            barrier,
            inc=1,
            device_id={"aux": aux, "orb": flip(orb, k, orb_count)},
            device_id_type=MESH,
        )
    for peer in (partner, across):
        pl.semaphore_signal(
            barrier, inc=1, device_id={"aux": peer, "orb": orb}, device_id_type=MESH
        )
    pl.semaphore_wait(barrier, orb_count + 1)

    steps = [(k, h) for k in spread_order(orb_count)[1:] + [1, 0] for h in range(parts)]

    def core_copy(k, h, side):
        row = y if side == 0 else 1 - y
        return pltpu.make_async_remote_copy(
            src_ref=r_ref.at[2 * row + 1 - core, flip(orb, k, orb_count), h],
            dst_ref=theirs.at[side, k, h],
            send_sem=c_send.at[side, k, h],
            recv_sem=c_recv.at[side, k, h],
            device_id={"aux": partner, "orb": orb},
            device_id_type=MESH,
        )

    def load(k, h, side, slot):
        row = y if side == 0 else 1 - y
        return pltpu.make_async_copy(
            r_ref.at[2 * row + core, flip(orb, k, orb_count), h],
            mine.at[slot, side],
            load_sem.at[slot, side],
        )

    def y_copy(k, h):
        return pltpu.make_async_remote_copy(
            src_ref=sums.at[1, k, h],
            dst_ref=peer_sums.at[k, h],
            send_sem=y_send.at[k, h],
            recv_sem=y_recv.at[k, h],
            device_id={"aux": across, "orb": orb},
            device_id_type=MESH,
        )

    def orb_copy(k, h):
        return pltpu.make_async_remote_copy(
            src_ref=sums.at[0, k, h],
            dst_ref=out_ref.at[orb, h],
            send_sem=orb_send.at[k, h],
            recv_sem=orb_recv.at[k, h],
            device_id={"aux": aux, "orb": flip(orb, k, orb_count)},
            device_id_type=MESH,
        )

    def keep(h):
        return pltpu.make_async_copy(sums.at[0, 0, h], out_ref.at[orb, h], keep_sem.at[h])

    def add(into, left, right):
        def one(i, carry):
            at = pl.ds(pl.multiple_of(i * tile, tile), tile)
            into[at, :] = left[at, :] + right[at, :]
            return carry

        lax.fori_loop(0, rows // tile, one, 0)

    def finish(k, h):
        y_copy(k, h).wait_recv()
        add(sums.at[0, k, h], sums.at[0, k, h], peer_sums.at[k, h])
        if k:
            orb_copy(k, h).start()
        else:
            keep(h).start()

    for k, h in steps:
        for side in (1, 0):
            core_copy(k, h, side).start()
    for side in (1, 0):
        load(*steps[0], side, 0).start()
    pending = []
    for place, (k, h) in enumerate(steps):
        slot = place % 2
        if place + 1 < len(steps):
            for side in (1, 0):
                load(*steps[place + 1], side, 1 - slot).start()
        for side in (1, 0):
            core_copy(k, h, side).wait_recv()
            load(k, h, side, slot).wait()
            add(sums.at[side, k, h], mine.at[slot, side], theirs.at[side, k, h])
            if side == 1:
                y_copy(k, h).start()
        pending.append((k, h))
        if len(pending) > 2:
            finish(*pending.pop(0))
    for unit in pending:
        finish(*unit)
    for k, h in steps:
        for side in (1, 0):
            core_copy(k, h, side).wait_send()
        y_copy(k, h).wait_send()
        if k:
            orb_copy(k, h).wait()
        else:
            keep(h).wait()


def give_back(contributions, collective_id):
    orb_count, parts, rows, cols = contributions.shape[1:]
    whole = (orb_count, parts, rows, cols)
    dma = pltpu.SemaphoreType.DMA
    return pl.pallas_call(
        functools.partial(return_kernel, orb_count),
        out_shape=jax.ShapeDtypeStruct(whole, f32),
        in_specs=[pl.BlockSpec(memory_space=pl.ANY)],
        out_specs=pl.BlockSpec(memory_space=pl.ANY),
        scratch_shapes=[
            pltpu.VMEM((2, 2, rows, cols), f32),
            pltpu.VMEM((2,) + whole, f32),
            pltpu.VMEM((2,) + whole, f32),
            pltpu.VMEM(whole, f32),
            dma((2, 2)),
            dma((2, orb_count, parts)),
            dma((2, orb_count, parts)),
            dma((orb_count, parts)),
            dma((orb_count, parts)),
            dma((orb_count, parts)),
            dma((orb_count, parts)),
            dma((parts,)),
        ],
        compiler_params=pltpu.CompilerParams(
            collective_id=collective_id, has_side_effects=True, vmem_limit_bytes=VMEM_LIMIT
        ),
        name="give_back",
    )(contributions)


def amplitude_kernel(
    first_ref, second_ref, shift_ref, left, right, col, row, upper, lower, total
):
    pair = pl.program_id(0)
    step = pl.program_id(1)

    @pl.when(step == 0)
    def _():
        total[...] = jnp.zeros_like(total)

    total[...] += dot3(split(left[0, 0]), split(right[0, 0]), ((0,), (0,)))

    @pl.when(step == pl.num_programs(1) - 1)
    def _():
        amps = -total[...] / (col[...] + row[...] - shift_ref[pair])
        upper[0], lower[0] = split(amps)


def amplitudes_of(first_slot, second_slot, shift, slots, vir_energy):
    pairs = first_slot.shape[0]
    aux_count, _, rows, cols = slots.shape
    return pl.pallas_call(
        amplitude_kernel,
        grid_spec=pltpu.PrefetchScalarGridSpec(
            num_scalar_prefetch=3,
            grid=(pairs, aux_count),
            in_specs=[
                pl.BlockSpec((1, 1, rows, cols), lambda p, a, f, s, e: (a, f[p], 0, 0)),
                pl.BlockSpec((1, 1, rows, cols), lambda p, a, f, s, e: (a, s[p], 0, 0)),
                pl.BlockSpec((cols, 1), lambda p, a, f, s, e: (0, 0)),
                pl.BlockSpec((1, cols), lambda p, a, f, s, e: (0, 0)),
            ],
            out_specs=[pl.BlockSpec((1, cols, cols), lambda p, a, f, s, e: (p, 0, 0))] * 2,
            scratch_shapes=[pltpu.VMEM((cols, cols), f32)],
        ),
        out_shape=[jax.ShapeDtypeStruct((pairs, cols, cols), bf16)] * 2,
        compiler_params=pltpu.CompilerParams(vmem_limit_bytes=VMEM_LIMIT),
        name="pair_amplitudes",
    )(first_slot, second_slot, shift, slots, slots, vir_energy[:, None], vir_energy[None, :])


def contribution_kernel(first_ref, second_ref, slots, upper, lower, out):
    slot = pl.program_id(1)
    out[0, 0] = jnp.zeros_like(out[0, 0])

    def visit(pair, carry):
        first = first_ref[pair]
        second = second_ref[pair]

        @pl.when(first == slot)
        def _():
            out[0, 0] += dot3(
                split(slots[0, second]), (upper[pair], lower[pair]), ((1,), (1,))
            )

        @pl.when(second == slot)
        def _():
            out[0, 0] += dot3(
                split(slots[0, first]), (upper[pair], lower[pair]), ((1,), (0,))
            )

        return carry

    lax.fori_loop(0, upper.shape[0], visit, 0)


def contributions_of(first_slot, second_slot, slots, amps):
    aux_count, orb_count, rows, cols = slots.shape
    return pl.pallas_call(
        contribution_kernel,
        grid_spec=pltpu.PrefetchScalarGridSpec(
            num_scalar_prefetch=2,
            grid=(aux_count, orb_count),
            in_specs=[
                pl.BlockSpec((1, orb_count, rows, cols), lambda a, o, f, s: (a, 0, 0, 0)),
                pl.BlockSpec(amps[0].shape, lambda a, o, f, s: (0, 0, 0)),
                pl.BlockSpec(amps[1].shape, lambda a, o, f, s: (0, 0, 0)),
            ],
            out_specs=pl.BlockSpec((1, 1, rows, cols), lambda a, o, f, s: (a, o, 0, 0)),
        ),
        out_shape=jax.ShapeDtypeStruct(slots.shape, f32),
        compiler_params=pltpu.CompilerParams(vmem_limit_bytes=VMEM_LIMIT),
        name="slot_contributions",
    )(first_slot, second_slot, slots, *amps)


def body(integrals, metric, occ_energy, vir_energy, pair_orbitals):
    aux_rows, occ_count, vir_count = integrals.shape
    aux_count = lax.axis_size("aux")
    orb_count = lax.axis_size("orb")
    aux_index = lax.axis_index("aux")
    orb_index = lax.axis_index("orb")
    pieces = 8
    pieced = (4, aux_rows // 4, vir_count)
    columns = occ_count * vir_count
    all_rows = gather(
        integrals.reshape(pieces, 1, aux_rows // pieces, columns), aux_count, False, 1
    ).reshape(aux_count * aux_rows, columns)
    fitted = lax.dot_general(
        metric, all_rows, (((1,), (0,)), ((), ())), precision=high, preferred_element_type=f32
    )
    pair_count = pair_orbitals.shape[0] // orb_count
    pair_ends = pair_orbitals.reshape(orb_count, 2 * pair_count)
    local_pick = jnp.where(pair_ends // occ_count == orb_index, pair_ends % occ_count, -1)
    wanted = jnp.max(local_pick, axis=1)
    parted = [
        fitted[:, o * vir_count : (o + 1) * vir_count].reshape(pieced) for o in range(occ_count)
    ]

    def choose(picked):
        total = jnp.zeros(picked.shape + pieced, f32)
        for o in range(occ_count):
            total = jnp.where((picked == o)[:, None, None, None], parted[o][None], total)
        return total

    if orb_count == 8 and occ_count < 4:
        half = jnp.stack([flip(orb_index, k, 8) for k in range(4)])
        gate = flip(orb_index, 6, 8)
        gate_pick = jnp.where(pair_ends // occ_count == gate, pair_ends % occ_count, -1)
        gate_wanted = jnp.max(gate_pick, axis=1)[half]
        hits = (gate_wanted[:, None] == jnp.arange(occ_count, dtype=jnp.int32)[None, :]).astype(f32)
        slots = gateway_exchange(hits, jnp.stack(parted), choose(wanted[half]), 2)
    else:
        slots = gather(choose(wanted), aux_count, True, 2)
    slots = slots.reshape(aux_count, orb_count, aux_rows, vir_count)
    my_count = pair_count // aux_count
    my_pairs = lax.dynamic_slice_in_dim(
        pair_orbitals, orb_index * pair_count + aux_index * my_count, my_count, 0
    )
    first_orb = my_pairs[:, 0]
    second_orb = my_pairs[:, 1]
    first_slot = first_orb // occ_count
    second_slot = second_orb // occ_count
    shift = occ_energy[first_orb] + occ_energy[second_orb]
    amps = amplitudes_of(first_slot, second_slot, shift, slots, vir_energy)
    contributions = contributions_of(first_slot, second_slot, slots, amps)
    received = give_back(contributions.reshape((aux_count, orb_count) + pieced), 3)
    received = received.reshape(orb_count, aux_rows, vir_count)
    keep = wanted[:, None] == jnp.arange(occ_count, dtype=jnp.int32)[None, :]
    return jnp.sum(
        jnp.where(keep[:, None, :, None], received[:, :, None, :], 0.0), axis=0
    )


def plain_body(integrals, metric, occ_energy, vir_energy, pair_orbitals):
    aux_rows, occ_count, vir_count = integrals.shape
    flat_rows = integrals.reshape(aux_rows, occ_count * vir_count)
    fitted = lax.psum_scatter(
        lax.dot_general(
            metric, flat_rows, (((0,), (0,)), ((), ())), precision=high, preferred_element_type=f32
        ),
        "aux",
        scatter_dimension=0,
        tiled=True,
    )
    fitted = fitted.reshape(aux_rows, occ_count, vir_count)
    orb_count = lax.axis_size("orb")
    my_index = lax.axis_index("orb")
    pair_count = pair_orbitals.shape[0] // orb_count
    pair_ends = pair_orbitals.reshape(orb_count, 2 * pair_count)
    local_pick = jnp.where(pair_ends // occ_count == my_index, pair_ends % occ_count, -1)
    wanted = jnp.max(local_pick, axis=1)
    chooser = (wanted[:, None] == jnp.arange(occ_count, dtype=jnp.int32)[None, :]).astype(f32)
    outgoing = jnp.einsum("to,qoa->qta", chooser, fitted, precision=high)
    arrived = lax.all_to_all(outgoing, "orb", split_axis=1, concat_axis=1, tiled=True)
    my_pairs = lax.dynamic_slice_in_dim(pair_orbitals, my_index * pair_count, pair_count, 0)
    first_orb = my_pairs[:, 0]
    second_orb = my_pairs[:, 1]
    first_slot = first_orb // occ_count
    second_slot = second_orb // occ_count
    left_block = jnp.take(arrived, first_slot, axis=1)
    right_block = jnp.take(arrived, second_slot, axis=1)
    partial_sums = jnp.einsum("qpa,qpb->pab", left_block, right_block, precision=high)
    occ_shift = occ_energy[first_orb] + occ_energy[second_orb]
    amp_share = lax.psum_scatter(partial_sums, "aux", scatter_dimension=1, tiled=True)
    share_rows = amp_share.shape[1]
    part_vir = lax.dynamic_slice_in_dim(
        vir_energy, lax.axis_index("aux") * share_rows, share_rows, 0
    )
    denominator = part_vir[None, :, None] + vir_energy[None, None, :] - occ_shift[:, None, None]
    amplitudes = lax.all_gather(-amp_share / denominator, "aux", axis=1, tiled=True)
    to_first = jnp.einsum("qpb,pab->qpa", right_block, amplitudes, precision=high)
    to_second = jnp.einsum("qpa,pab->qpb", left_block, amplitudes, precision=high)
    slot_ids = jnp.arange(orb_count, dtype=jnp.int32)
    first_hits = (first_slot[:, None] == slot_ids[None, :]).astype(f32)
    second_hits = (second_slot[:, None] == slot_ids[None, :]).astype(f32)
    return_slots = jnp.einsum("qpa,ps->qsa", to_first, first_hits, precision=high)
    return_slots = return_slots + jnp.einsum(
        "qpa,ps->qsa", to_second, second_hits, precision=high
    )
    received = lax.all_to_all(return_slots, "orb", split_axis=1, concat_axis=1, tiled=True)
    return jnp.einsum("qta,to->qoa", received, chooser, precision=high)


def solution(mesh):
    aux_count = mesh.shape["aux"]
    orb_count = mesh.shape["orb"]

    def step(integrals, metric, occ_energy, vir_energy, pair_orbitals):
        slot_bytes = 4 * metric.shape[1] * integrals.shape[2] * orb_count
        fits = 2 * slot_bytes <= 64 * 1024 * 1024
        power = orb_count & (orb_count - 1) == 0
        whole_pairs = pair_orbitals.shape[0] % (orb_count * aux_count) == 0
        chosen = body if fits and power and whole_pairs and aux_count == 4 else plain_body
        return jax.shard_map(
            chosen,
            mesh=mesh,
            in_specs=(P("aux", "orb", None), P("aux", None), P(), P(), P()),
            out_specs=P("aux", "orb", None),
            check_vma=False,
        )(integrals, metric, occ_energy, vir_energy, pair_orbitals)

    return step
```

```python
import functools

import jax
import jax.numpy as jnp
from jax import lax
from jax.experimental import pallas as pl
from jax.experimental.pallas import tpu as pltpu
from jax.sharding import PartitionSpec as P

high = lax.Precision.HIGH
MESH = pl.DeviceIdType.MESH
VMEM_LIMIT = 60 * 1024 * 1024
f32 = jnp.float32
bf16 = jnp.bfloat16


def flip(index, step, count):
    total = 0
    bit = 1
    while bit < count:
        total = total + bit * ((index // bit + (step // bit) % 2) % 2)
        bit *= 2
    return total


def spread_order(count):
    far = list(range(count // 2, count))
    near = list(range(2, count // 2))
    far = far[0::2] + far[1::2]
    merged = [1]
    while far or near:
        if far:
            merged.append(far.pop(0))
        if near:
            merged.append(near.pop(0))
    return merged


def split(value):
    upper = value.astype(bf16)
    lower = (value - upper.astype(f32)).astype(bf16)
    return upper, lower


def dot3(left, right, dims):
    (lu, ll), (ru, rl) = left, right
    (la,), (ra,) = dims
    return lax.dot_general(
        jnp.concatenate([lu, lu, ll], axis=la),
        jnp.concatenate([ru, rl, ru], axis=ra),
        (dims, ((), ())),
        preferred_element_type=f32,
    )


def gather_kernel(
    orb_count,
    y_count,
    exchange,
    x_ref,
    out_ref,
    stage,
    keep_sem,
    orb_send,
    orb_recv,
    y_send,
    y_recv,
    c_send,
    c_recv,
):
    aux = lax.axis_index("aux")
    orb = lax.axis_index("orb")
    y = aux // 2
    core = aux % 2
    partner = 2 * y + 1 - core
    blocks = x_ref.shape[0]

    def y_peer(j):
        return 2 * ((y + j) % y_count) + core

    barrier = pltpu.get_barrier_semaphore()
    greeted = 0
    if exchange:
        for k in range(1, orb_count):
            pl.semaphore_signal(
                barrier,
                inc=1,
                device_id={"aux": aux, "orb": flip(orb, k, orb_count)},
                device_id_type=MESH,
            )
            greeted += 1
    for j in range(1, y_count):
        pl.semaphore_signal(
            barrier, inc=1, device_id={"aux": y_peer(j), "orb": orb}, device_id_type=MESH
        )
        greeted += 1
    pl.semaphore_signal(
        barrier, inc=1, device_id={"aux": partner, "orb": orb}, device_id_type=MESH
    )
    greeted += 1
    pl.semaphore_wait(barrier, greeted)

    def orb_copy(k, h):
        to = flip(orb, k, orb_count)
        return pltpu.make_async_remote_copy(
            src_ref=x_ref.at[to, h],
            dst_ref=out_ref.at[aux, orb, h],
            send_sem=orb_send.at[k, h],
            recv_sem=orb_recv.at[k, h],
            device_id={"aux": aux, "orb": to},
            device_id_type=MESH,
        )

    def place_of(k):
        return flip(orb, k, orb_count) if exchange else k

    def own(k, h):
        if not exchange or k == 0:
            return x_ref.at[place_of(k), h]
        return out_ref.at[aux, place_of(k), h]

    def y_copy(k, h, j):
        return pltpu.make_async_remote_copy(
            src_ref=own(k, h),
            dst_ref=out_ref.at[aux, place_of(k), h],
            send_sem=y_send.at[j - 1, k, h],
            recv_sem=y_recv.at[j - 1, k, h],
            device_id={"aux": y_peer(j), "orb": orb},
            device_id_type=MESH,
        )

    def core_copy(k, h):
        return pltpu.make_async_remote_copy(
            src_ref=own(k, h),
            dst_ref=out_ref.at[aux, place_of(k), h],
            send_sem=c_send.at[0, k, h],
            recv_sem=c_recv.at[0, k, h],
            device_id={"aux": partner, "orb": orb},
            device_id_type=MESH,
        )

    def relay_copy(k, h, j):
        source = 2 * ((y + y_count - j) % y_count) + core
        return pltpu.make_async_remote_copy(
            src_ref=out_ref.at[source, place_of(k), h],
            dst_ref=out_ref.at[source, place_of(k), h],
            send_sem=c_send.at[j, k, h],
            recv_sem=c_recv.at[j, k, h],
            device_id={"aux": partner, "orb": orb},
            device_id_type=MESH,
        )

    steps = spread_order(orb_count) if exchange else list(range(1, blocks))
    units = [(k, h) for k in [0] + steps for h in range(x_ref.shape[1])]
    if exchange:
        for k, h in units:
            if k:
                orb_copy(k, h).start()
    pending = []

    def relay(k, h):
        for j in range(1, y_count):
            y_copy(k, h, j).wait_recv()
            relay_copy(k, h, j).start()

    def keep_loads():
        return [
            pltpu.make_async_copy(own(k, h), stage.at[i], keep_sem.at[i])
            for i, (k, h) in enumerate(keeps)
        ]

    def keep_saves():
        return [
            pltpu.make_async_copy(stage.at[i], out_ref.at[aux, place_of(k), h], keep_sem.at[i])
            for i, (k, h) in enumerate(keeps)
        ]

    keeps = [(k, h) for k, h in units if k == 0 or not exchange]
    for copy in keep_loads():
        copy.start()
    for index, (k, h) in enumerate(units):
        if exchange and k:
            orb_copy(k, h).wait_recv()
        for j in range(1, y_count):
            y_copy(k, h, j).start()
        core_copy(k, h).start()
        pending.append((k, h))
        if len(pending) > 2:
            relay(*pending.pop(0))
        if index == len(keeps) - 1:
            for load, save in zip(keep_loads(), keep_saves()):
                load.wait()
                save.start()
    for unit in pending:
        relay(*unit)
    for k, h in units:
        core_copy(k, h).wait()
        for j in range(1, y_count):
            relay_copy(k, h, j).wait()
            y_copy(k, h, j).wait_send()
        if exchange and k:
            orb_copy(k, h).wait_send()
    for save in keep_saves():
        save.wait()


def gather(blocks, aux_count, exchange, collective_id):
    count, parts = blocks.shape[:2]
    y_count = aux_count // 2
    kept = parts if exchange else count * parts
    dma = pltpu.SemaphoreType.DMA
    return pl.pallas_call(
        functools.partial(gather_kernel, count, y_count, exchange),
        out_shape=jax.ShapeDtypeStruct((aux_count,) + blocks.shape, f32),
        in_specs=[pl.BlockSpec(memory_space=pl.ANY)],
        out_specs=pl.BlockSpec(memory_space=pl.ANY),
        scratch_shapes=[
            pltpu.VMEM((kept,) + blocks.shape[2:], f32),
            dma((kept,)),
            dma((count, parts)),
            dma((count, parts)),
            dma((y_count - 1, count, parts)),
            dma((y_count - 1, count, parts)),
            dma((y_count, count, parts)),
            dma((y_count, count, parts)),
        ],
        compiler_params=pltpu.CompilerParams(
            collective_id=collective_id, has_side_effects=True, vmem_limit_bytes=VMEM_LIMIT
        ),
        name="gather_exchange" if exchange else "gather_aux",
    )(blocks)


def return_kernel(
    orb_count,
    r_ref,
    out_ref,
    mine,
    theirs,
    sums,
    peer_sums,
    load_sem,
    c_send,
    c_recv,
    y_send,
    y_recv,
    orb_send,
    orb_recv,
    keep_sem,
):
    aux = lax.axis_index("aux")
    orb = lax.axis_index("orb")
    y = aux // 2
    core = aux % 2
    partner = 2 * y + 1 - core
    across = 2 * (1 - y) + core
    parts, rows = r_ref.shape[2:4]
    tile = 64

    barrier = pltpu.get_barrier_semaphore()
    for k in range(1, orb_count):
        pl.semaphore_signal(
            barrier,
            inc=1,
            device_id={"aux": aux, "orb": flip(orb, k, orb_count)},
            device_id_type=MESH,
        )
    for peer in (partner, across):
        pl.semaphore_signal(
            barrier, inc=1, device_id={"aux": peer, "orb": orb}, device_id_type=MESH
        )
    pl.semaphore_wait(barrier, orb_count + 1)

    steps = [(k, h) for k in spread_order(orb_count)[1:] + [1, 0] for h in range(parts)]

    def core_copy(k, h, side):
        row = y if side == 0 else 1 - y
        return pltpu.make_async_remote_copy(
            src_ref=r_ref.at[2 * row + 1 - core, flip(orb, k, orb_count), h],
            dst_ref=theirs.at[side, k, h],
            send_sem=c_send.at[side, k, h],
            recv_sem=c_recv.at[side, k, h],
            device_id={"aux": partner, "orb": orb},
            device_id_type=MESH,
        )

    def load(k, h, side, slot):
        row = y if side == 0 else 1 - y
        return pltpu.make_async_copy(
            r_ref.at[2 * row + core, flip(orb, k, orb_count), h],
            mine.at[slot, side],
            load_sem.at[slot, side],
        )

    def y_copy(k, h):
        return pltpu.make_async_remote_copy(
            src_ref=sums.at[1, k, h],
            dst_ref=peer_sums.at[k, h],
            send_sem=y_send.at[k, h],
            recv_sem=y_recv.at[k, h],
            device_id={"aux": across, "orb": orb},
            device_id_type=MESH,
        )

    def orb_copy(k, h):
        return pltpu.make_async_remote_copy(
            src_ref=sums.at[0, k, h],
            dst_ref=out_ref.at[orb, h],
            send_sem=orb_send.at[k, h],
            recv_sem=orb_recv.at[k, h],
            device_id={"aux": aux, "orb": flip(orb, k, orb_count)},
            device_id_type=MESH,
        )

    def keep(h):
        return pltpu.make_async_copy(sums.at[0, 0, h], out_ref.at[orb, h], keep_sem.at[h])

    def add(into, left, right):
        def one(i, carry):
            at = pl.ds(pl.multiple_of(i * tile, tile), tile)
            into[at, :] = left[at, :] + right[at, :]
            return carry

        lax.fori_loop(0, rows // tile, one, 0)

    def finish(k, h):
        y_copy(k, h).wait_recv()
        add(sums.at[0, k, h], sums.at[0, k, h], peer_sums.at[k, h])
        if k:
            orb_copy(k, h).start()
        else:
            keep(h).start()

    for k, h in steps:
        for side in (1, 0):
            core_copy(k, h, side).start()
    for side in (1, 0):
        load(*steps[0], side, 0).start()
    pending = []
    for place, (k, h) in enumerate(steps):
        slot = place % 2
        if place + 1 < len(steps):
            for side in (1, 0):
                load(*steps[place + 1], side, 1 - slot).start()
        for side in (1, 0):
            core_copy(k, h, side).wait_recv()
            load(k, h, side, slot).wait()
            add(sums.at[side, k, h], mine.at[slot, side], theirs.at[side, k, h])
            if side == 1:
                y_copy(k, h).start()
        pending.append((k, h))
        if len(pending) > 2:
            finish(*pending.pop(0))
    for unit in pending:
        finish(*unit)
    for k, h in steps:
        for side in (1, 0):
            core_copy(k, h, side).wait_send()
        y_copy(k, h).wait_send()
        if k:
            orb_copy(k, h).wait()
        else:
            keep(h).wait()


def give_back(contributions, collective_id):
    orb_count, parts, rows, cols = contributions.shape[1:]
    whole = (orb_count, parts, rows, cols)
    dma = pltpu.SemaphoreType.DMA
    return pl.pallas_call(
        functools.partial(return_kernel, orb_count),
        out_shape=jax.ShapeDtypeStruct(whole, f32),
        in_specs=[pl.BlockSpec(memory_space=pl.ANY)],
        out_specs=pl.BlockSpec(memory_space=pl.ANY),
        scratch_shapes=[
            pltpu.VMEM((2, 2, rows, cols), f32),
            pltpu.VMEM((2,) + whole, f32),
            pltpu.VMEM((2,) + whole, f32),
            pltpu.VMEM(whole, f32),
            dma((2, 2)),
            dma((2, orb_count, parts)),
            dma((2, orb_count, parts)),
            dma((orb_count, parts)),
            dma((orb_count, parts)),
            dma((orb_count, parts)),
            dma((orb_count, parts)),
            dma((parts,)),
        ],
        compiler_params=pltpu.CompilerParams(
            collective_id=collective_id, has_side_effects=True, vmem_limit_bytes=VMEM_LIMIT
        ),
        name="give_back",
    )(contributions)


def amplitude_kernel(
    first_ref, second_ref, shift_ref, left, right, col, row, upper, lower, total
):
    pair = pl.program_id(0)
    step = pl.program_id(1)

    @pl.when(step == 0)
    def _():
        total[...] = jnp.zeros_like(total)

    total[...] += dot3(split(left[0, 0]), split(right[0, 0]), ((0,), (0,)))

    @pl.when(step == pl.num_programs(1) - 1)
    def _():
        amps = -total[...] / (col[...] + row[...] - shift_ref[pair])
        upper[0], lower[0] = split(amps)


def amplitudes_of(first_slot, second_slot, shift, slots, vir_energy):
    pairs = first_slot.shape[0]
    aux_count, _, rows, cols = slots.shape
    return pl.pallas_call(
        amplitude_kernel,
        grid_spec=pltpu.PrefetchScalarGridSpec(
            num_scalar_prefetch=3,
            grid=(pairs, aux_count),
            in_specs=[
                pl.BlockSpec((1, 1, rows, cols), lambda p, a, f, s, e: (a, f[p], 0, 0)),
                pl.BlockSpec((1, 1, rows, cols), lambda p, a, f, s, e: (a, s[p], 0, 0)),
                pl.BlockSpec((cols, 1), lambda p, a, f, s, e: (0, 0)),
                pl.BlockSpec((1, cols), lambda p, a, f, s, e: (0, 0)),
            ],
            out_specs=[pl.BlockSpec((1, cols, cols), lambda p, a, f, s, e: (p, 0, 0))] * 2,
            scratch_shapes=[pltpu.VMEM((cols, cols), f32)],
        ),
        out_shape=[jax.ShapeDtypeStruct((pairs, cols, cols), bf16)] * 2,
        compiler_params=pltpu.CompilerParams(vmem_limit_bytes=VMEM_LIMIT),
        name="pair_amplitudes",
    )(first_slot, second_slot, shift, slots, slots, vir_energy[:, None], vir_energy[None, :])


def contribution_kernel(first_ref, second_ref, slots, upper, lower, out):
    slot = pl.program_id(1)
    out[0, 0] = jnp.zeros_like(out[0, 0])

    def visit(pair, carry):
        first = first_ref[pair]
        second = second_ref[pair]

        @pl.when(first == slot)
        def _():
            out[0, 0] += dot3(
                split(slots[0, second]), (upper[pair], lower[pair]), ((1,), (1,))
            )

        @pl.when(second == slot)
        def _():
            out[0, 0] += dot3(
                split(slots[0, first]), (upper[pair], lower[pair]), ((1,), (0,))
            )

        return carry

    lax.fori_loop(0, upper.shape[0], visit, 0)


def contributions_of(first_slot, second_slot, slots, amps):
    aux_count, orb_count, rows, cols = slots.shape
    return pl.pallas_call(
        contribution_kernel,
        grid_spec=pltpu.PrefetchScalarGridSpec(
            num_scalar_prefetch=2,
            grid=(aux_count, orb_count),
            in_specs=[
                pl.BlockSpec((1, orb_count, rows, cols), lambda a, o, f, s: (a, 0, 0, 0)),
                pl.BlockSpec(amps[0].shape, lambda a, o, f, s: (0, 0, 0)),
                pl.BlockSpec(amps[1].shape, lambda a, o, f, s: (0, 0, 0)),
            ],
            out_specs=pl.BlockSpec((1, 1, rows, cols), lambda a, o, f, s: (a, o, 0, 0)),
        ),
        out_shape=jax.ShapeDtypeStruct(slots.shape, f32),
        compiler_params=pltpu.CompilerParams(vmem_limit_bytes=VMEM_LIMIT),
        name="slot_contributions",
    )(first_slot, second_slot, slots, *amps)


def body(integrals, metric, occ_energy, vir_energy, pair_orbitals):
    aux_rows, occ_count, vir_count = integrals.shape
    aux_count = lax.axis_size("aux")
    orb_count = lax.axis_size("orb")
    aux_index = lax.axis_index("aux")
    orb_index = lax.axis_index("orb")
    pieces = 8
    halves = (4, aux_rows // 4, vir_count)
    columns = occ_count * vir_count
    all_rows = gather(
        integrals.reshape(pieces, 1, aux_rows // pieces, columns), aux_count, False, 1
    ).reshape(aux_count * aux_rows, columns)
    fitted = lax.dot_general(
        metric, all_rows, (((1,), (0,)), ((), ())), precision=high, preferred_element_type=f32
    )
    pair_count = pair_orbitals.shape[0] // orb_count
    pair_ends = pair_orbitals.reshape(orb_count, 2 * pair_count)
    local_pick = jnp.where(pair_ends // occ_count == orb_index, pair_ends % occ_count, -1)
    wanted = jnp.max(local_pick, axis=1)
    outgoing = jnp.zeros((orb_count, aux_rows, vir_count), f32)
    for o in range(occ_count):
        part = fitted[:, o * vir_count : (o + 1) * vir_count]
        outgoing = jnp.where((wanted == o)[:, None, None], part[None], outgoing)
    slots = gather(outgoing.reshape((orb_count,) + halves), aux_count, True, 2)
    slots = slots.reshape(aux_count, orb_count, aux_rows, vir_count)
    my_count = pair_count // aux_count
    my_pairs = lax.dynamic_slice_in_dim(
        pair_orbitals, orb_index * pair_count + aux_index * my_count, my_count, 0
    )
    first_orb = my_pairs[:, 0]
    second_orb = my_pairs[:, 1]
    first_slot = first_orb // occ_count
    second_slot = second_orb // occ_count
    shift = occ_energy[first_orb] + occ_energy[second_orb]
    amps = amplitudes_of(first_slot, second_slot, shift, slots, vir_energy)
    contributions = contributions_of(first_slot, second_slot, slots, amps)
    received = give_back(contributions.reshape((aux_count, orb_count) + halves), 3)
    received = received.reshape(orb_count, aux_rows, vir_count)
    outs = [
        jnp.sum(jnp.where((wanted == o)[:, None, None], received, 0.0), axis=0)
        for o in range(occ_count)
    ]
    return jnp.stack(outs, axis=1)


def plain_body(integrals, metric, occ_energy, vir_energy, pair_orbitals):
    aux_rows, occ_count, vir_count = integrals.shape
    flat_rows = integrals.reshape(aux_rows, occ_count * vir_count)
    fitted = lax.psum_scatter(
        lax.dot_general(
            metric, flat_rows, (((0,), (0,)), ((), ())), precision=high, preferred_element_type=f32
        ),
        "aux",
        scatter_dimension=0,
        tiled=True,
    )
    fitted = fitted.reshape(aux_rows, occ_count, vir_count)
    orb_count = lax.axis_size("orb")
    my_index = lax.axis_index("orb")
    pair_count = pair_orbitals.shape[0] // orb_count
    pair_ends = pair_orbitals.reshape(orb_count, 2 * pair_count)
    local_pick = jnp.where(pair_ends // occ_count == my_index, pair_ends % occ_count, -1)
    wanted = jnp.max(local_pick, axis=1)
    chooser = (wanted[:, None] == jnp.arange(occ_count, dtype=jnp.int32)[None, :]).astype(f32)
    outgoing = jnp.einsum("to,qoa->qta", chooser, fitted, precision=high)
    arrived = lax.all_to_all(outgoing, "orb", split_axis=1, concat_axis=1, tiled=True)
    my_pairs = lax.dynamic_slice_in_dim(pair_orbitals, my_index * pair_count, pair_count, 0)
    first_orb = my_pairs[:, 0]
    second_orb = my_pairs[:, 1]
    first_slot = first_orb // occ_count
    second_slot = second_orb // occ_count
    left_block = jnp.take(arrived, first_slot, axis=1)
    right_block = jnp.take(arrived, second_slot, axis=1)
    partial_sums = jnp.einsum("qpa,qpb->pab", left_block, right_block, precision=high)
    occ_shift = occ_energy[first_orb] + occ_energy[second_orb]
    amp_share = lax.psum_scatter(partial_sums, "aux", scatter_dimension=1, tiled=True)
    share_rows = amp_share.shape[1]
    part_vir = lax.dynamic_slice_in_dim(
        vir_energy, lax.axis_index("aux") * share_rows, share_rows, 0
    )
    denominator = part_vir[None, :, None] + vir_energy[None, None, :] - occ_shift[:, None, None]
    amplitudes = lax.all_gather(-amp_share / denominator, "aux", axis=1, tiled=True)
    to_first = jnp.einsum("qpb,pab->qpa", right_block, amplitudes, precision=high)
    to_second = jnp.einsum("qpa,pab->qpb", left_block, amplitudes, precision=high)
    slot_ids = jnp.arange(orb_count, dtype=jnp.int32)
    first_hits = (first_slot[:, None] == slot_ids[None, :]).astype(f32)
    second_hits = (second_slot[:, None] == slot_ids[None, :]).astype(f32)
    return_slots = jnp.einsum("qpa,ps->qsa", to_first, first_hits, precision=high)
    return_slots = return_slots + jnp.einsum(
        "qpa,ps->qsa", to_second, second_hits, precision=high
    )
    received = lax.all_to_all(return_slots, "orb", split_axis=1, concat_axis=1, tiled=True)
    return jnp.einsum("qta,to->qoa", received, chooser, precision=high)


def solution(mesh):
    aux_count = mesh.shape["aux"]
    orb_count = mesh.shape["orb"]

    def step(integrals, metric, occ_energy, vir_energy, pair_orbitals):
        slot_bytes = 4 * metric.shape[1] * integrals.shape[2] * orb_count
        fits = 2 * slot_bytes <= 64 * 1024 * 1024
        power = orb_count & (orb_count - 1) == 0
        whole_pairs = pair_orbitals.shape[0] % (orb_count * aux_count) == 0
        chosen = body if fits and power and whole_pairs and aux_count == 4 else plain_body
        return jax.shard_map(
            chosen,
            mesh=mesh,
            in_specs=(P("aux", "orb", None), P("aux", None), P(), P(), P()),
            out_specs=P("aux", "orb", None),
            check_vma=False,
        )(integrals, metric, occ_energy, vir_energy, pair_orbitals)

    return step
```
